32 devices in a mesh: dp: 4 (over x, core), seq: 4 (over z), tensor: 2 (over y).
Axes of the slice: x: 2, y: 2, z: 4, core: 2. Of those that a mesh axis runs over, the one named last changes fastest.
Arguments:
- queries: bfloat16 [4, 2048, 1024], P('dp', 'seq', 'tensor'), may hold values from -6 to 6
- key_vectors: bfloat16 [4, 2048, 1024], P('dp', 'seq', 'tensor'), may hold values from -6 to 6
- value_vectors: bfloat16 [4, 2048, 1024], P('dp', 'seq', 'tensor'), may hold values from -6 to 6
- log_decay: float32 [4, 8, 2048], P('dp', 'tensor'), may hold values from -0.75 to 0
- w_out: bfloat16 [1024, 3072], P('tensor'), may hold values from -0.1875 to 0.1875
- grad_out: bfloat16 [4, 2048, 3072], P('dp', 'seq', 'tensor'), may hold values from -6 to 6
Outputs:
- grad_queries: bfloat16 [4, 2048, 1024], P('dp', 'seq', 'tensor')
- grad_keys: bfloat16 [4, 2048, 1024], P('dp', 'seq', 'tensor')
- grad_values: bfloat16 [4, 2048, 1024], P('dp', 'seq', 'tensor')
- grad_w_t: float32 [3072, 1024], P(('dp', 'seq'), 'tensor')
The draws below stay inside these ranges and needn't reach their ends.
All inputs are finite; a program needn't handle non-finite values.
Results may differ from the reference program's by a relative error of at most 0.015.
Values may be sent and summed in bfloat16 or wider, within the bound.
No kernel may reach another device: no remote copies, remote signals or barrier semaphores. Data moves between devices by JAX's collectives and lax.ppermute only.
A program may use at most 64 MiB of HBM per device.

```python
import math
import jax
import jax.numpy as jnp
from jax import lax

D = 3072
HD = 128
HEADS_DEV = 4
TOK_DEV = 512
MICRO = 1
HEADS = 8
F = 1024
TOKEN_SPAN = 2048
BATCH = 4
N_DP = 4
N_SEQ = 4


def draw_log_decay(key, part):
    interval_portions = jax.random.split(key, 10)
    entire_dimensions = (BATCH, HEADS, TOKEN_SPAN)
    head_shape = (BATCH, HEADS, 1)
    block_count = TOKEN_SPAN // TOK_DEV
    slow_share = 1.0 / 3.0
    medium_share = 0.5
    group_pick = jax.random.randint(interval_portions[0], (BATCH, HEADS // HEADS_DEV, 1), 0, HEADS_DEV)
    head_place = lax.broadcasted_iota(jnp.int32, head_shape, 1) % HEADS_DEV
    forced = head_place == jnp.repeat(group_pick, HEADS_DEV, axis=1)
    category = jax.random.uniform(interval_portions[1], head_shape, dtype=jnp.float32)
    slow_heads = forced | (category < slow_share)
    medium_heads = jnp.logical_not(slow_heads) & (category < slow_share + medium_share)
    slow_rate = jnp.exp(jax.random.uniform(interval_portions[2], head_shape, dtype=jnp.float32, minval=math.log(0.1 / TOKEN_SPAN), maxval=math.log(0.5 / TOKEN_SPAN)))
    medium_rate = jnp.exp(jax.random.uniform(interval_portions[3], head_shape, dtype=jnp.float32, minval=math.log(0.05 / TOK_DEV), maxval=math.log(0.2 / TOK_DEV)))
    fast_rate = jnp.exp(jax.random.uniform(interval_portions[4], head_shape, dtype=jnp.float32, minval=math.log(1.0 / 50.0), maxval=math.log(1.0 / 30.0)))
    head_rate = jnp.where(slow_heads, slow_rate, jnp.where(medium_heads, medium_rate, fast_rate))
    forgetting_noise = jax.random.uniform(interval_portions[5], entire_dimensions, dtype=jnp.float32, minval=0.5, maxval=1.5)
    run_start = jax.random.randint(interval_portions[6], (BATCH, HEADS, block_count), TOK_DEV // 4, 3 * TOK_DEV // 4 - 5)
    start_spread = jnp.repeat(run_start, TOK_DEV, axis=2)
    inner_pos = lax.broadcasted_iota(jnp.int32, entire_dimensions, 2) % TOK_DEV
    in_run = medium_heads & (inner_pos >= start_spread) & (inner_pos < start_spread + 5)
    run_total = jax.random.uniform(interval_portions[7], (BATCH, HEADS, block_count), dtype=jnp.float32, minval=-3.6, maxval=-3.25)
    run_spread = jnp.repeat(run_total, TOK_DEV, axis=2)
    spike_clusters = (jax.random.uniform(interval_portions[8], entire_dimensions, dtype=jnp.float32) < 3.0 / TOKEN_SPAN) & jnp.logical_not(in_run)
    kept_proportion = jax.random.uniform(interval_portions[9], entire_dimensions, dtype=jnp.float32, minval=0.5, maxval=0.8)
    base_part = -head_rate * forgetting_noise
    run_part = jnp.where(in_run, run_spread / 5.0, 0.0)
    spike_part = jnp.where(spike_clusters, jnp.log(kept_proportion), 0.0)
    return base_part + run_part + spike_part


def with_spikes(result, stream_key, source, target, parts, factor):
    def block_of(dim):
        return (jnp.arange(result.shape[dim]) // (result.shape[dim] // parts)).reshape((-1,) + (1,) * (result.ndim - 1 - dim))

    one_side = jax.random.permutation(stream_key, parts)[block_of(target)]
    second = (block_of(target) + parts // 2) % parts
    return jnp.where((block_of(source) == one_side) | (block_of(source) == second), factor * result, result)


def level_of(stream_key, extent, shards, least, top_value):
    level, own = 1.0, jax.random.fold_in(stream_key, 6)
    for axis_at, shards_of in shards:
        draws = jnp.exp(jax.random.uniform(jax.random.fold_in(own, axis_at), (shards_of,), jnp.float32, least / len(shards), top_value / len(shards)))
        level = level * jnp.repeat(draws, extent[axis_at] // shards_of).reshape([-1 if axis == axis_at else 1 for axis in range(len(extent))])
    return level


def scatter_about(own_key, extent, width, limit, cuts=(), held_as=jnp.bfloat16):
    gain = level_of(own_key, extent, cuts, -0.22, 0.18) if cuts else 1.0
    entries = jax.random.normal(own_key, extent, jnp.float32) * width * gain
    return jnp.minimum(jnp.maximum(entries, -limit), limit).astype(held_as)


def gaussian_with(rng, extent, deviation, most, pieces, heavy, kind=jnp.bfloat16):
    values = deviation * jax.random.normal(rng, extent, jnp.float32)
    if pieces:
        values = values * level_of(rng, extent, pieces, -0.22, 0.18)
    return jnp.clip(with_spikes(values, jax.random.fold_in(rng, 3), *heavy), -most, most).astype(kind)


def setup_inputs(seed: int = 0) -> dict:
    key_of = jax.random.split(jax.random.key(seed), 7)
    queries = scatter_about(key_of[0], (BATCH, TOKEN_SPAN, F), 1.0, 6.0, ((0, 4), (1, 4), (2, 2)))
    key_vectors = scatter_about(key_of[1], (BATCH, TOKEN_SPAN, F), 1.0, 6.0, ((0, 4), (1, 4), (2, 2)))
    value_vectors = scatter_about(key_of[2], (BATCH, TOKEN_SPAN, F), 1.0, 6.0, ((0, 4), (1, 4), (2, 2)))
    log_decay = draw_log_decay(jax.random.fold_in(key_of[6], 71), 0)
    w_out = scatter_about(key_of[4], (F, D), F ** -0.5, 0.1875, ((0, 2),))
    grad_out = gaussian_with(key_of[5], (BATCH, TOKEN_SPAN, D), 1.0, 6.0, ((0, 4), (1, 4), (2, 2)), (1, 2, 4, 2.0))
    return {"queries": queries, "key_vectors": key_vectors, "value_vectors": value_vectors, "log_decay": log_decay, "w_out": w_out, "grad_out": grad_out}


highest_precision = lax.Precision.HIGHEST

def decay_matrix(cumulative):
    size_now = cumulative.shape[-1]
    later_pos = lax.broadcasted_iota(jnp.int32, (size_now, size_now), 0)
    earlier_pos = lax.broadcasted_iota(jnp.int32, (size_now, size_now), 1)
    lower = later_pos >= earlier_pos
    spread = cumulative[..., :, None] - cumulative[..., None, :]
    return jnp.where(lower, jnp.exp(jnp.where(lower, spread, 0.0)), 0.0)

def block_terms(decay_block):
    cumulative = jnp.cumsum(decay_block, axis=2)
    block_total = cumulative[:, :, -1]
    decay_mask = decay_matrix(cumulative)
    from_start = jnp.transpose(jnp.exp(cumulative), (0, 2, 1))[..., None]
    to_end = jnp.transpose(jnp.exp(block_total[:, :, None] - cumulative), (0, 2, 1))[..., None]
    return (block_total, decay_mask, from_start, to_end)

def reference(queries, key_vectors, value_vectors, log_decay, w_out, grad_out):
    batch_count, length, features = queries.shape
    head_count = features // HD
    blocks = length // TOK_DEV
    inverse = 1.0 / HD
    grad_scale = 1.0 / math.sqrt(batch_count * length)
    grad_attn = jnp.dot(grad_out.reshape(batch_count * length, D), w_out.T, preferred_element_type=jnp.float32)
    grad_attn = grad_attn.astype(jnp.bfloat16).reshape(batch_count, length, features)

    def blocked(tensor):
        return jnp.transpose(tensor.reshape(batch_count, blocks, TOK_DEV, head_count, HD), (1, 0, 2, 3, 4))
    decays = jnp.transpose(log_decay.reshape(batch_count, head_count, blocks, TOK_DEV), (2, 0, 1, 3))
    query_blocks = blocked(queries)
    key_blocks = blocked(key_vectors)
    value_blocks = blocked(value_vectors)
    grad_blocks = blocked(grad_attn)

    def forward_step(state_now, inputs):
        query_block, key_block, value_block, decay_block = inputs
        block_total, decay_mask, from_start, to_end = block_terms(decay_block)
        query_float = query_block.astype(jnp.float32)
        key_float = key_block.astype(jnp.float32)
        value_float = value_block.astype(jnp.float32)
        scores = jnp.einsum('bthd,bshd->bhts', query_float, key_float)
        weights = (scores * decay_mask * inverse).astype(jnp.bfloat16)
        within_block = jnp.einsum('bhts,bshd->bthd', weights.astype(jnp.float32), value_float)
        from_carried = jnp.einsum('bthd,bhde->bthe', query_float * from_start, state_now, precision=highest_precision)
        attn_block = (within_block + from_carried * inverse).astype(jnp.bfloat16)
        update = jnp.einsum('bshd,bshe->bhde', key_float * to_end, value_float, precision=highest_precision)
        new_state = jnp.exp(block_total)[:, :, None, None] * state_now + update
        return (new_state, (attn_block, state_now))
    initial = jnp.zeros((batch_count, head_count, HD, HD), jnp.float32)
    final_state, (attn_blocks, carried) = lax.scan(forward_step, initial, (query_blocks, key_blocks, value_blocks, decays))
    attn_out = jnp.transpose(attn_blocks, (1, 0, 2, 3, 4)).reshape(batch_count, length, features)

    def backward_step(back_state, inputs):
        query_block, key_block, value_block, decay_block, grad_block, state_now = inputs
        block_total, decay_mask, from_start, to_end = block_terms(decay_block)
        query_float = query_block.astype(jnp.float32)
        key_float = key_block.astype(jnp.float32)
        value_float = value_block.astype(jnp.float32)
        grad_float = grad_block.astype(jnp.float32)
        scores = jnp.einsum('bthd,bshd->bhts', query_float, key_float)
        weights = (scores * decay_mask * inverse).astype(jnp.bfloat16).astype(jnp.float32)
        grad_scores = jnp.einsum('bthd,bshd->bhts', grad_float, value_float)
        grad_weights = (grad_scores * decay_mask * inverse).astype(jnp.bfloat16).astype(jnp.float32)
        grad_query = jnp.einsum('bhts,bshd->bthd', grad_weights, key_float) + jnp.einsum('bthe,bhde->bthd', grad_float * from_start, state_now, precision=highest_precision) * inverse
        grad_key = jnp.einsum('bhts,bthd->bshd', grad_weights, query_float) + jnp.einsum('bshe,bhde->bshd', value_float * to_end, back_state, precision=highest_precision)
        grad_value = jnp.einsum('bhts,bthd->bshd', weights, grad_float) + jnp.einsum('bshd,bhde->bshe', key_float * to_end, back_state, precision=highest_precision)
        local_back = jnp.einsum('bthd,bthe->bhde', query_float * from_start, grad_float, precision=highest_precision) * inverse
        new_back = jnp.exp(block_total)[:, :, None, None] * back_state + local_back
        return (new_back, (grad_query.astype(jnp.bfloat16), grad_key.astype(jnp.bfloat16), grad_value.astype(jnp.bfloat16)))
    final_back, (grad_q_blocks, grad_k_blocks, grad_v_blocks) = lax.scan(backward_step, initial, (query_blocks, key_blocks, value_blocks, decays, grad_blocks, carried), reverse=True)

    def unblocked(tensor):
        return jnp.transpose(tensor, (1, 0, 2, 3, 4)).reshape(batch_count, length, features)

    def add_partial(running, group_index):
        replica = (group_index // N_SEQ).astype(jnp.int32)
        seq_block = (group_index % N_SEQ).astype(jnp.int32)
        zero_index = jnp.zeros((), jnp.int32)
        grad_rows = lax.dynamic_slice(grad_out, (replica * MICRO, seq_block * TOK_DEV, zero_index), (MICRO, TOK_DEV, D)).reshape(MICRO * TOK_DEV, D)
        attn_rows = lax.dynamic_slice(attn_out, (replica * MICRO, seq_block * TOK_DEV, zero_index), (MICRO, TOK_DEV, features)).reshape(MICRO * TOK_DEV, features)
        partial_sum = jnp.dot(grad_rows.T, attn_rows, preferred_element_type=jnp.float32) * grad_scale
        rounded = lax.optimization_barrier(partial_sum.astype(jnp.bfloat16)).astype(jnp.float32)
        return (running + rounded, None)
    grad_w_t, unused_tail = lax.scan(add_partial, jnp.zeros((D, features), jnp.float32), jnp.arange(N_DP * N_SEQ, dtype=jnp.int32))
    return (unblocked(grad_q_blocks), unblocked(grad_k_blocks), unblocked(grad_v_blocks), grad_w_t)
```

```python
import functools
import math

import jax
import jax.numpy as jnp
from jax import lax
from jax.experimental import pallas as pl
from jax.experimental.pallas import tpu as pltpu
from jax.sharding import PartitionSpec as P

F32 = jnp.float32
BF16 = jnp.bfloat16
TILE = 256


def dot_nn(a, b):
    return lax.dot_general(a, b, (((1,), (0,)), ((), ())), preferred_element_type=F32)


def dot_nt(a, b):
    return lax.dot_general(a, b, (((1,), (1,)), ((), ())), preferred_element_type=F32)


def dot_tn(a, b):
    return lax.dot_general(a, b, (((0,), (0,)), ((), ())), preferred_element_type=F32)


def call(body, outs, args, scratch=(), scalars=None, grid=None, in_specs=None, out_specs=None):
    count = 0 if scalars is None else 1
    whole = pl.BlockSpec(memory_space=pltpu.VMEM)
    spec = pltpu.PrefetchScalarGridSpec(
        num_scalar_prefetch=count,
        grid=grid or (),
        in_specs=in_specs or [whole] * len(args),
        out_specs=out_specs or [whole] * len(outs),
        scratch_shapes=list(scratch),
    )
    prefix = () if scalars is None else (scalars,)
    return pl.pallas_call(body, out_shape=list(outs), grid_spec=spec)(*prefix, *args)


def shape(dims, kind):
    return jax.ShapeDtypeStruct(dims, kind)


def running_sum(values):
    length = values.shape[1]
    position = lax.broadcasted_iota(jnp.int32, values.shape, 1)
    step = 1
    while step < length:
        values = values + jnp.where(position >= step, pltpu.roll(values, step, 1), 0.0)
        step *= 2
    return values


def span_decay(decay_ref, start, stop):
    values = decay_ref[...]
    position = lax.broadcasted_iota(jnp.int32, values.shape, 1)
    inside = (position >= start) & (position < stop)
    return jnp.exp(jnp.sum(jnp.where(inside, values, 0.0), axis=1, keepdims=True))


def states_kernel(place, decay_ref, key_ref, value_ref, state_ref, row_ref, column_ref, *, heads):
    rows = key_ref.shape[0]
    width = key_ref.shape[1] // heads
    local = decay_ref[:, pl.ds(pl.multiple_of(place[0] * rows, 128), rows)]
    tall = -(-heads // 8) * 8
    local = jnp.concatenate([local] * (tall // heads), axis=0) if tall % heads == 0 else jnp.pad(local, ((0, tall - heads), (0, 0)))
    cumulative = running_sum(local)
    columns = cumulative.T
    row_ref[...] = cumulative
    column_ref[...] = columns
    for h in range(heads):
        at = slice(h * width, (h + 1) * width)
        to_end = jnp.exp(cumulative[h : h + 1, rows - 1 : rows] - columns[:, h : h + 1])
        scaled = (key_ref[:, at].astype(F32) * to_end).astype(BF16)
        state_ref[h] = dot_tn(scaled, value_ref[:, at]).astype(BF16)


def tiles(rows):
    return [(i, j) for i in range(rows // TILE) for j in range(i + 1)]


def tile_decay(row_ref, column_ref, h, i, j):
    spread = column_ref[i * TILE : (i + 1) * TILE, h : h + 1] - row_ref[h : h + 1, j * TILE : (j + 1) * TILE]
    if i != j:
        return jnp.exp(spread)
    later = lax.broadcasted_iota(jnp.int32, (TILE, TILE), 0)
    earlier = lax.broadcasted_iota(jnp.int32, (TILE, TILE), 1)
    lower = later >= earlier
    return jnp.where(lower, jnp.exp(jnp.where(lower, spread, 0.0)), 0.0)


def weights_kernel(query_ref, key_ref, value_ref, row_ref, column_ref, weight_ref, within_ref, *, heads):
    rows = key_ref.shape[0]
    width = key_ref.shape[1] // heads
    for h in range(heads):
        at = slice(h * width, (h + 1) * width)
        sums = {}
        for n, (i, j) in enumerate(tiles(rows)):
            ti, tj = slice(i * TILE, (i + 1) * TILE), slice(j * TILE, (j + 1) * TILE)
            scores = dot_nt(query_ref[ti, at], key_ref[tj, at])
            weight = (scores * tile_decay(row_ref, column_ref, h, i, j) * (1.0 / width)).astype(BF16)
            weight_ref[h, n] = weight
            term = dot_nn(weight, value_ref[tj, at])
            sums[i] = term if i not in sums else sums[i] + term
        for i, total in sums.items():
            within_ref[i * TILE : (i + 1) * TILE, at] = total


def gather_states(decay_ref, pieces, place, rows, forward):
    factors = []
    for k in range(2, len(pieces) + 1):
        start = (place - k + 1) * rows if forward else (place + 1) * rows
        stop = place * rows if forward else (place + k) * rows
        factors.append(span_decay(decay_ref, start, stop))

    def state(h):
        total = pieces[0][h].astype(F32)
        for factor, piece in zip(factors, pieces[1:], strict=True):
            total = total + factor[h : h + 1] * piece[h].astype(F32)
        return total.astype(BF16)

    return state


def attention_kernel(place, decay_ref, query_ref, within_ref, column_ref, *refs, heads):
    *pieces, attn_ref, carried_ref = refs
    rows = query_ref.shape[0]
    width = query_ref.shape[1] // heads
    state = gather_states(decay_ref, pieces, place[0], rows, True)
    for h in range(heads):
        at = slice(h * width, (h + 1) * width)
        carried = state(h)
        carried_ref[h] = carried
        scaled = query_ref[:, at].astype(F32) * (jnp.exp(column_ref[:, h : h + 1]) * (1.0 / width))
        attn_ref[:, at] = (within_ref[:, at] + dot_nn(scaled.astype(BF16), carried)).astype(BF16)


def projection_kernel(place, grad_ref, attn_ref, send_ref, keep_ref, *, scale):
    part = (dot_tn(grad_ref[...], attn_ref[...]) * scale).astype(BF16)

    @pl.when(pl.program_id(0) == 0)
    def _():
        send_ref[...] = part

    @pl.when(pl.program_id(0) == 1)
    def _():
        keep_ref[...] = part


def grad_attn_half_kernel(place, grad_ref, out_ref, total_ref):
    total_ref[...] = dot_nt(grad_ref[...], out_ref[...])


def grad_attn_kernel(place, grad_ref, out_ref, half_ref, query_ref, column_ref, grad_attn_ref, back_ref, *, heads):
    width = query_ref.shape[1] // heads
    total = half_ref[...] + dot_nt(grad_ref[...], out_ref[...])
    total = total.astype(BF16)
    grad_attn_ref[...] = total
    for h in range(heads):
        at = slice(h * width, (h + 1) * width)
        scaled = query_ref[:, at].astype(F32) * (jnp.exp(column_ref[:, h : h + 1]) * (1.0 / width))
        back_ref[h] = dot_tn(scaled.astype(BF16), total[:, at]).astype(BF16)


def inner_kernel(
    query_ref, key_ref, value_ref, grad_ref, row_ref, column_ref, weight_ref, carried_ref, dq_ref, dk_ref, dv_ref, *, heads
):
    rows = key_ref.shape[0]
    width = key_ref.shape[1] // heads
    inverse = 1.0 / width
    for h in range(heads):
        at = slice(h * width, (h + 1) * width)
        dq, dk, dv = {}, {}, {}

        def add(store, index, term):
            store[index] = term if index not in store else store[index] + term

        for n, (i, j) in enumerate(tiles(rows)):
            ti, tj = slice(i * TILE, (i + 1) * TILE), slice(j * TILE, (j + 1) * TILE)
            scores = dot_nt(grad_ref[ti, at], value_ref[tj, at])
            weight = (scores * tile_decay(row_ref, column_ref, h, i, j) * inverse).astype(BF16)
            add(dq, i, dot_nn(weight, key_ref[tj, at]))
            add(dk, j, dot_tn(weight, query_ref[ti, at]))
            add(dv, j, dot_tn(weight_ref[h, n], grad_ref[ti, at]))
        for i in range(rows // TILE):
            ti = slice(i * TILE, (i + 1) * TILE)
            scaled = grad_ref[ti, at].astype(F32) * (jnp.exp(column_ref[ti, h : h + 1]) * inverse)
            dq_ref[ti, at] = (dq[i] + dot_nt(scaled.astype(BF16), carried_ref[h])).astype(BF16)
            dk_ref[ti, at] = dk[i]
            dv_ref[ti, at] = dv[i]


def outer_kernel(place, decay_ref, key_ref, value_ref, row_ref, column_ref, inner_k_ref, inner_v_ref, *refs, heads):
    *pieces, dk_ref, dv_ref = refs
    rows = key_ref.shape[0]
    width = key_ref.shape[1] // heads
    state = gather_states(decay_ref, pieces, place[0], rows, False)
    for h in range(heads):
        at = slice(h * width, (h + 1) * width)
        back = state(h)
        to_end = jnp.exp(row_ref[h : h + 1, rows - 1 : rows] - column_ref[:, h : h + 1])
        values = (value_ref[:, at].astype(F32) * to_end).astype(BF16)
        keys = (key_ref[:, at].astype(F32) * to_end).astype(BF16)
        dk_ref[:, at] = (inner_k_ref[:, at] + dot_nt(values, back)).astype(BF16)
        dv_ref[:, at] = (inner_v_ref[:, at] + dot_nn(keys, back)).astype(BF16)


def pieces_kernel(place, keep_ref, other_ref, own_ref, *send_refs):
    count = len(send_refs) + 1
    rows = own_ref.shape[0]
    for k in range(count):
        at = pl.ds(pl.multiple_of(lax.rem(place[0] + k, count) * rows, 16), rows)
        total = keep_ref[at, :].astype(F32) + other_ref[at, :].astype(F32)
        if k == 0:
            own_ref[...] = total
        else:
            send_refs[k - 1][...] = total.astype(BF16)


def finish_kernel(place, *refs):
    *pieces, send_ref, keep_ref = refs
    half = len(pieces) // 2

    def total(group):
        value = group[0][...]
        for piece in group[1:]:
            value = value + piece[...].astype(F32)
        return value

    first, second = total(pieces[:half]), total(pieces[half:])
    mine = place[2] == place[3]
    send_ref[...] = jnp.where(mine, second, first).astype(BF16)
    keep_ref[...] = jnp.where(mine, first, second)


def shift_up(value, count):
    return [lax.ppermute(value, "seq", [(i, i + k) for i in range(count - k)]) for k in range(1, count)]


def shift_down(value, count):
    return [lax.ppermute(value, "seq", [(i, i - k) for i in range(k, count)]) for k in range(1, count)]


def swap(value, axis, bit):
    return lax.ppermute(value, axis, [(i, i ^ bit) for i in range(lax.axis_size(axis))])


def local(queries, key_vectors, value_vectors, log_decay, w_out, grad_out):
    micro, rows, features = queries.shape
    heads = log_decay.shape[1]
    width = features // heads
    dp_count, seq_count, tensor_count = (lax.axis_size(n) for n in ("dp", "seq", "tensor"))
    seq_index, dp_index, tensor_index = (lax.axis_index(n) for n in ("seq", "dp", "tensor"))
    scale = 1.0 / math.sqrt(micro * dp_count * rows * seq_count)
    query, key, value = queries[0], key_vectors[0], value_vectors[0]
    decay, grad = log_decay[0], grad_out[0]
    columns = grad.shape[1]
    model = columns * tensor_count
    paired = tensor_count == 2 and dp_count == 2 * tensor_count
    place = jnp.stack([seq_index, dp_index % 2, dp_index // 2, tensor_index]).astype(jnp.int32)
    tall = -(-heads // 8) * 8
    state_shape = shape((heads, width, width), BF16)
    token_f32, token_bf16 = shape((rows, features), F32), shape((rows, features), BF16)

    if paired:
        other = swap(grad, "tensor", 1)
    else:
        other = lax.all_gather(grad, "tensor", axis=1, tiled=True)

    state, row, column = call(
        functools.partial(states_kernel, heads=heads),
        [state_shape, shape((tall, rows), F32), shape((rows, tall), F32)],
        [decay, key, value],
        scalars=place,
    )
    received = shift_up(state, seq_count)
    weight, within = call(
        functools.partial(weights_kernel, heads=heads),
        [shape((heads, len(tiles(rows)), TILE, TILE), BF16), token_f32],
        [query, key, value, row, column],
    )
    attn, carried = call(
        functools.partial(attention_kernel, heads=heads),
        [token_bf16, state_shape],
        [decay, query, within, column, *received],
        scalars=place,
    )

    def blocks(wide, tall_part, index):
        return pl.BlockSpec((wide, tall_part), lambda i, p: (0, index(i, p)))

    if paired:
        dest = columns // 2
        piece = dest // seq_count

        def project(gradient):
            send, keep = call(
                functools.partial(projection_kernel, scale=scale),
                [shape((dest, features), BF16)] * 2,
                [gradient, attn],
                scalars=place,
                grid=(2,),
                in_specs=[
                    pl.BlockSpec((rows, dest), lambda i, p: (0, jnp.where(i == 0, 1 - p[1], p[1]))),
                    pl.BlockSpec((rows, features), lambda i, p: (0, 0)),
                ],
                out_specs=[pl.BlockSpec((dest, features), lambda i, p: (0, 0))] * 2,
            )
            came = swap(send, "dp", 1)
            own, *sends = call(
                pieces_kernel,
                [shape((piece, features), F32)] + [shape((piece, features), BF16)] * (seq_count - 1),
                [keep, came],
                scalars=place,
            )
            parts = [own]
            for k, part in enumerate(sends, 1):
                parts.append(lax.ppermute(part, "seq", [(i, (i + k) % seq_count) for i in range(seq_count)]))
            return parts

        first = project(grad)
        half_in = [
            pl.BlockSpec((rows, columns), lambda i, p: (0, 0)),
            pl.BlockSpec((features, columns), lambda i, p: (0, p[3])),
        ]
        (half,) = call(
            grad_attn_half_kernel, [token_f32], [grad, w_out], scalars=place, grid=(1,), in_specs=half_in,
            out_specs=[pl.BlockSpec((rows, features), lambda i, p: (0, 0))],
        )
        second = project(other)
        far = pl.BlockSpec((features, columns), lambda i, p: (0, 1 - p[3]))
    else:
        partial = (dot_tn(other, attn) * scale).astype(BF16)
        grad_w = lax.psum_scatter(partial, ("dp", "seq"), scatter_dimension=0, tiled=True).astype(F32)
        half = jnp.zeros((rows, features), F32)
        far = pl.BlockSpec((features, model), lambda i, p: (0, 0))

    def flat(*dims):
        return pl.BlockSpec(dims, lambda i, p: (0,) * len(dims))

    grad_attn, back = call(
        functools.partial(grad_attn_kernel, heads=heads),
        [token_bf16, state_shape],
        [other, w_out, half, query, column],
        scalars=place,
        grid=(1,),
        in_specs=[flat(*other.shape), far, flat(rows, features), flat(rows, features), flat(rows, tall)],
        out_specs=[flat(rows, features), flat(heads, width, width)],
    )
    returned = shift_down(back, seq_count)
    grad_queries, inner_keys, inner_values = call(
        functools.partial(inner_kernel, heads=heads),
        [token_bf16, token_f32, token_f32],
        [query, key, value, grad_attn, row, column, weight, carried],
    )
    grad_keys, grad_values = call(
        functools.partial(outer_kernel, heads=heads),
        [token_bf16, token_bf16],
        [decay, key, value, row, column, inner_keys, inner_values, *returned],
        scalars=place,
    )
    if paired:
        send, keep = call(
            finish_kernel,
            [shape((piece, features), BF16), shape((piece, features), F32)],
            [*first, *second],
            scalars=place,
        )
        grad_w = keep + swap(send, "dp", 2).astype(F32)
    return grad_queries[None], grad_keys[None], grad_values[None], grad_w


def solution(mesh):
    tokens = P("dp", "seq", "tensor")
    in_specs = (tokens, tokens, tokens, P("dp", "tensor", None), P("tensor", None), tokens)
    out_specs = (tokens, tokens, tokens, P(("dp", "seq"), "tensor"))
    return jax.shard_map(local, mesh=mesh, in_specs=in_specs, out_specs=out_specs, check_vma=False)
```

```python
import functools
import math

import jax
import jax.numpy as jnp
from jax import lax
from jax.experimental import pallas as pl
from jax.experimental.pallas import tpu as pltpu
from jax.sharding import PartitionSpec as P


F32 = jnp.float32
BF16 = jnp.bfloat16
TILE = 256
GRANT = 24 * 1024 * 1024


def dot_nn(a, b):
    return lax.dot_general(a, b, (((1,), (0,)), ((), ())), preferred_element_type=F32)


def dot_nt(a, b):
    return lax.dot_general(a, b, (((1,), (1,)), ((), ())), preferred_element_type=F32)


def dot_tn(a, b):
    return lax.dot_general(a, b, (((0,), (0,)), ((), ())), preferred_element_type=F32)


def call(body, outs, args, scalars=None, scratch=(), near=True):
    count = 0 if scalars is None else 1
    whole = pl.BlockSpec(memory_space=pltpu.VMEM)
    given = whole if near else pl.BlockSpec(memory_space=pltpu.HBM)
    spec = pltpu.PrefetchScalarGridSpec(
        num_scalar_prefetch=count,
        in_specs=[given] * len(args),
        out_specs=[whole] * len(outs),
        scratch_shapes=list(scratch),
    )
    prefix = () if scalars is None else (scalars,)
    args = [pltpu.with_memory_space_constraint(x, pltpu.VMEM if near else pltpu.HBM) for x in args]
    limit = pltpu.CompilerParams(vmem_limit_bytes=GRANT)
    return pl.pallas_call(body, out_shape=list(outs), grid_spec=spec, compiler_params=limit)(*prefix, *args)


def after(value, *others):
    return lax.optimization_barrier((value, *others))[0]


def shape(dims, kind):
    return pltpu.VMEM(dims, kind)


def final(dims, kind):
    return jax.ShapeDtypeStruct(dims, kind)


def running_sum(values):
    length = values.shape[1]
    position = lax.broadcasted_iota(jnp.int32, values.shape, 1)
    step = 1
    while step < length:
        values = values + jnp.where(position >= step, pltpu.roll(values, step, 1), 0.0)
        step *= 2
    return values


def span_decay(decay_ref, start, stop):
    values = decay_ref[...]
    position = lax.broadcasted_iota(jnp.int32, values.shape, 1)
    inside = (position >= start) & (position < stop)
    return jnp.exp(jnp.sum(jnp.where(inside, values, 0.0), axis=1, keepdims=True))


def states_kernel(place, decay_in, query_in, key_in, value_in, *refs, heads):
    outs, (semaphores,) = refs[:-1], refs[-1:]
    state_ref, row_ref, column_ref, decay_ref, query_ref, key_ref, value_ref = outs
    pairs = ((decay_in, decay_ref), (key_in, key_ref), (value_in, value_ref), (query_in, query_ref))
    copies = [pltpu.make_async_copy(*pair, semaphores.at[n]) for n, pair in enumerate(pairs)]
    for copy in copies:
        copy.start()
    rows = key_ref.shape[0]
    width = key_ref.shape[1] // heads
    copies[0].wait()
    local = decay_ref[:, pl.ds(pl.multiple_of(place[0] * rows, 128), rows)]
    tall = row_ref.shape[0]
    local = jnp.concatenate([local] * pl.cdiv(tall, heads), axis=0)[:tall]
    cumulative = running_sum(local)
    columns = cumulative.T
    row_ref[...] = cumulative
    column_ref[...] = columns
    copies[1].wait()
    copies[2].wait()
    for h in range(heads):
        at = slice(h * width, (h + 1) * width)
        to_end = jnp.exp(cumulative[h : h + 1, rows - 1 : rows] - columns[:, h : h + 1])
        scaled = (key_ref[:, at].astype(F32) * to_end).astype(BF16)
        state_ref[h] = dot_tn(scaled, value_ref[:, at]).astype(BF16)
    copies[3].wait()


def tiles(rows):
    return [(i, j) for i in range(rows // TILE) for j in range(i + 1)]


def tile_decay(row_ref, column_ref, h, i, j):
    spread = column_ref[i * TILE : (i + 1) * TILE, h : h + 1] - row_ref[h : h + 1, j * TILE : (j + 1) * TILE]
    if i != j:
        return jnp.exp(spread)
    later = lax.broadcasted_iota(jnp.int32, (TILE, TILE), 0)
    earlier = lax.broadcasted_iota(jnp.int32, (TILE, TILE), 1)
    lower = later >= earlier
    return jnp.where(lower, jnp.exp(jnp.where(lower, spread, 0.0)), 0.0)


def weights_kernel(query_ref, key_ref, value_ref, row_ref, column_ref, weight_ref, within_ref, *, heads):
    rows = key_ref.shape[0]
    width = key_ref.shape[1] // heads
    for h in range(heads):
        at = slice(h * width, (h + 1) * width)
        sums = {}
        for n, (i, j) in enumerate(tiles(rows)):
            ti, tj = slice(i * TILE, (i + 1) * TILE), slice(j * TILE, (j + 1) * TILE)
            scores = dot_nt(query_ref[ti, at], key_ref[tj, at])
            weight = (scores * tile_decay(row_ref, column_ref, h, i, j) * (1.0 / width)).astype(BF16)
            weight_ref[h, n] = weight
            term = dot_nn(weight, value_ref[tj, at])
            sums[i] = term if i not in sums else sums[i] + term
        for i, total in sums.items():
            within_ref[i * TILE : (i + 1) * TILE, at] = total


def gather_states(decay_ref, pieces, place, rows, forward):
    factors = []
    for k in range(2, len(pieces) + 1):
        start = (place - k + 1) * rows if forward else (place + 1) * rows
        stop = place * rows if forward else (place + k) * rows
        factors.append(span_decay(decay_ref, start, stop))

    def state(h):
        total = pieces[0][h].astype(F32)
        for factor, piece in zip(factors, pieces[1:], strict=True):
            total = total + factor[h : h + 1] * piece[h].astype(F32)
        return total.astype(BF16)

    return state


def attend(place, decay_ref, query_ref, within_ref, column_ref, pieces, attn_ref, carried_ref, heads):
    rows = query_ref.shape[0]
    width = query_ref.shape[1] // heads
    state = gather_states(decay_ref, pieces, place[0], rows, True)
    for h in range(heads):
        at = slice(h * width, (h + 1) * width)
        carried = state(h)
        carried_ref[h] = carried
        scaled = query_ref[:, at].astype(F32) * (jnp.exp(column_ref[:, h : h + 1]) * (1.0 / width))
        attn_ref[:, at] = (within_ref[:, at] + dot_nn(scaled.astype(BF16), carried)).astype(BF16)


def project(place, grad_ref, attn_ref, send_ref, keep_ref, scale):
    half = keep_ref.shape[0]
    for core, into in ((1 - place[1], send_ref), (place[1], keep_ref)):
        at = pl.ds(pl.multiple_of(core * half, 128), half)
        into[...] = (dot_tn(grad_ref[:, at], attn_ref[...]) * scale).astype(BF16)


def attention_kernel(place, decay_ref, query_ref, within_ref, column_ref, *refs, heads):
    *pieces, attn_ref, carried_ref = refs
    attend(place, decay_ref, query_ref, within_ref, column_ref, pieces, attn_ref, carried_ref, heads)


def attention_project_kernel(place, decay_ref, query_ref, within_ref, column_ref, grad_ref, *refs, heads, scale):
    *pieces, attn_ref, carried_ref, send_ref, keep_ref = refs
    attend(place, decay_ref, query_ref, within_ref, column_ref, pieces, attn_ref, carried_ref, heads)
    project(place, grad_ref, attn_ref, send_ref, keep_ref, scale)


def projection_kernel(place, grad_ref, attn_ref, send_ref, keep_ref, *, scale):
    project(place, grad_ref, attn_ref, send_ref, keep_ref, scale)


def half_columns(out_ref, index, count):
    return out_ref[:, pl.ds(pl.multiple_of(index * count, 128), count)]


def grad_attn_half_kernel(place, grad_ref, out_ref, total_ref):
    total_ref[...] = dot_nt(grad_ref[...], half_columns(out_ref, place[3], grad_ref.shape[1]))


def grad_attn_kernel(place, grad_ref, out_ref, query_ref, column_ref, *refs, heads):
    *halves, grad_attn_ref, back_ref = refs
    width = query_ref.shape[1] // heads
    if halves:
        total = halves[0][...] + dot_nt(grad_ref[...], half_columns(out_ref, 1 - place[3], grad_ref.shape[1]))
    else:
        total = dot_nt(grad_ref[...], out_ref[...])
    total = total.astype(BF16)
    grad_attn_ref[...] = total
    for h in range(heads):
        at = slice(h * width, (h + 1) * width)
        scaled = query_ref[:, at].astype(F32) * (jnp.exp(column_ref[:, h : h + 1]) * (1.0 / width))
        back_ref[h] = dot_tn(scaled.astype(BF16), total[:, at]).astype(BF16)


def inner_kernel(
    query_ref, key_ref, value_ref, grad_ref, row_ref, column_ref, weight_ref, carried_ref, dq_ref, dk_ref, dv_ref, *, heads
):
    rows = key_ref.shape[0]
    width = key_ref.shape[1] // heads
    inverse = 1.0 / width
    for h in range(heads):
        at = slice(h * width, (h + 1) * width)
        dq, dk, dv = {}, {}, {}

        def add(store, index, term):
            store[index] = term if index not in store else store[index] + term

        for n, (i, j) in enumerate(tiles(rows)):
            ti, tj = slice(i * TILE, (i + 1) * TILE), slice(j * TILE, (j + 1) * TILE)
            scores = dot_nt(grad_ref[ti, at], value_ref[tj, at])
            weight = (scores * tile_decay(row_ref, column_ref, h, i, j) * inverse).astype(BF16)
            add(dq, i, dot_nn(weight, key_ref[tj, at]))
            add(dk, j, dot_tn(weight, query_ref[ti, at]))
            add(dv, j, dot_tn(weight_ref[h, n], grad_ref[ti, at]))
        for i in range(rows // TILE):
            ti = slice(i * TILE, (i + 1) * TILE)
            scaled = grad_ref[ti, at].astype(F32) * (jnp.exp(column_ref[ti, h : h + 1]) * inverse)
            dq_ref[ti, at] = (dq[i] + dot_nt(scaled.astype(BF16), carried_ref[h])).astype(BF16)
            dk_ref[ti, at] = dk[i]
            dv_ref[ti, at] = dv[i]


def outer_kernel(place, decay_ref, key_ref, value_ref, row_ref, column_ref, inner_k_ref, inner_v_ref, *refs, heads):
    *pieces, dk_ref, dv_ref = refs
    rows = key_ref.shape[0]
    width = key_ref.shape[1] // heads
    state = gather_states(decay_ref, pieces, place[0], rows, False)
    for h in range(heads):
        at = slice(h * width, (h + 1) * width)
        back = state(h)
        to_end = jnp.exp(row_ref[h : h + 1, rows - 1 : rows] - column_ref[:, h : h + 1])
        values = (value_ref[:, at].astype(F32) * to_end).astype(BF16)
        keys = (key_ref[:, at].astype(F32) * to_end).astype(BF16)
        dk_ref[:, at] = (inner_k_ref[:, at] + dot_nt(values, back)).astype(BF16)
        dv_ref[:, at] = (inner_v_ref[:, at] + dot_nn(keys, back)).astype(BF16)


def pieces_kernel(place, mine_ref, other_ref, keep_ref, send_ref):
    rows = keep_ref.shape[1]
    for n in range(4):
        owner = place[0] ^ (2, 0, 3, 1)[n]
        at = pl.ds(pl.multiple_of(owner * rows, 16), rows)
        total = mine_ref[at, :].astype(F32) + other_ref[at, :].astype(F32)
        if n < 2:
            keep_ref[n] = total
        else:
            send_ref[n - 2] = total.astype(BF16)


def halve_kernel(mine_ref, other_ref, keep_ref, send_ref):
    send_ref[...] = (mine_ref[0] + other_ref[0].astype(F32)).astype(BF16)
    keep_ref[...] = mine_ref[1] + other_ref[1].astype(F32)


def finish_kernel(place, own_ref, own_other_ref, far_ref, far_other_ref, keep_ref, send_ref):
    first = own_ref[...] + own_other_ref[...].astype(F32)
    second = far_ref[...] + far_other_ref[...].astype(F32)
    mine = place[2] == place[3]
    send_ref[...] = jnp.where(mine, second, first).astype(BF16)
    keep_ref[...] = jnp.where(mine, first, second)


def shift_up(value, count):
    return [lax.ppermute(value, "seq", [(i, i + k) for i in range(count - k)]) for k in range(1, count)]


def shift_down(value, count):
    return [lax.ppermute(value, "seq", [(i, i - k) for i in range(k, count)]) for k in range(1, count)]


def swap(value, axis, bit):
    return lax.ppermute(value, axis, [(i, i ^ bit) for i in range(lax.axis_size(axis))])


def paired_mesh(dp_count, seq_count, tensor_count):
    return tensor_count == 2 and dp_count == 2 * tensor_count and seq_count == 4


def local(queries, key_vectors, value_vectors, log_decay, w_out, grad_out):
    micro, rows, features = queries.shape
    heads = log_decay.shape[1]
    width = features // heads
    dp_count, seq_count, tensor_count = (lax.axis_size(n) for n in ("dp", "seq", "tensor"))
    seq_index, dp_index, tensor_index = (lax.axis_index(n) for n in ("seq", "dp", "tensor"))
    scale = 1.0 / math.sqrt(micro * dp_count * rows * seq_count)
    query, key, value = queries[0], key_vectors[0], value_vectors[0]
    decay, grad = log_decay[0], grad_out[0]
    columns = grad.shape[1]
    paired = paired_mesh(dp_count, seq_count, tensor_count)
    place = jnp.stack([seq_index, dp_index % 2, dp_index // 2, tensor_index]).astype(jnp.int32)
    tall = -(-heads // 8) * 8
    state_shape = shape((heads, width, width), BF16)
    token_f32, token_bf16 = shape((rows, features), F32), shape((rows, features), BF16)

    if paired:
        other = swap(grad, "tensor", 1)
    else:
        other = lax.all_gather(grad, "tensor", axis=1, tiled=True)

    state, row, column, decay, query, key, value = call(
        functools.partial(states_kernel, heads=heads),
        [state_shape, shape((tall, rows), F32), shape((rows, tall), F32), shape(decay.shape, F32)] + [token_bf16] * 3,
        [decay, query, key, value],
        place,
        [pltpu.SemaphoreType.DMA((4,))],
        near=False,
    )
    received = shift_up(state, seq_count)
    weight, within = call(
        functools.partial(weights_kernel, heads=heads),
        [shape((heads, len(tiles(rows)), TILE, TILE), BF16), token_f32],
        [query, key, value, row, column],
    )
    attend_args = [decay, query, within, column]

    if paired:
        dest = columns // 2
        piece = dest // seq_count
        parts = [shape((dest, features), BF16)] * 2

        quarter = (piece, features)

        def spread(send, keep, *behind):
            came = swap(send, "dp", 1)
            stay, go = call(
                pieces_kernel,
                [shape((2, *quarter), F32), shape((2, *quarter), BF16)],
                [after(keep, *behind), came],
                place,
            )
            return stay, swap(go, "seq", 1)

        def halve(stay, came, *behind):
            stay, go = call(halve_kernel, [shape(quarter, F32), shape(quarter, BF16)], [after(stay, *behind), came])
            return stay, swap(go, "seq", 2)

        attn, carried, send, keep = call(
            functools.partial(attention_project_kernel, heads=heads, scale=scale),
            [token_bf16, state_shape, *parts],
            [*attend_args, grad, *received],
            place,
        )
        own_stay, own_came = spread(send, keep)
        (half,) = call(grad_attn_half_kernel, [token_f32], [grad, after(w_out, own_stay)], place)
        send, keep_far = call(
            functools.partial(projection_kernel, scale=scale), parts, [other, after(attn, half)], place
        )
        own_stay, own_came = halve(own_stay, own_came, keep_far)
        last = (half,)
    else:
        attn, carried = call(
            functools.partial(attention_kernel, heads=heads),
            [token_bf16, state_shape],
            [*attend_args, *received],
            place,
        )
        partial = (dot_tn(other, attn) * scale).astype(BF16)
        grad_w = lax.psum_scatter(partial, ("dp", "seq"), scatter_dimension=0, tiled=True).astype(F32)
        last, keep = (), attn

    if paired:
        keep = own_stay
    grad_attn, back = call(
        functools.partial(grad_attn_kernel, heads=heads),
        [token_bf16, state_shape],
        [other, w_out, after(query, keep), column, *last],
        place,
    )
    returned = shift_down(back, seq_count)
    if paired:
        far_stay, far_came = spread(send, keep_far, back)
        grad_attn = after(grad_attn, far_stay)
    grad_queries, inner_keys, inner_values = call(
        functools.partial(inner_kernel, heads=heads),
        [final((rows, features), BF16), token_f32, token_f32],
        [query, key, value, grad_attn, row, column, weight, carried],
    )
    if paired:
        far_stay, far_came = halve(far_stay, far_came, inner_keys)
        inner_keys = after(inner_keys, far_stay)
    grad_keys, grad_values = call(
        functools.partial(outer_kernel, heads=heads),
        [final((rows, features), BF16)] * 2,
        [decay, key, value, row, column, inner_keys, inner_values, *returned],
        place,
    )
    if paired:
        keep, send = call(
            finish_kernel,
            [shape(quarter, F32), shape(quarter, BF16)],
            [after(own_stay, grad_keys), own_came, far_stay, far_came],
            place,
        )
        grad_w = keep + swap(send, "dp", 2).astype(F32)
    return grad_queries[None], grad_keys[None], grad_values[None], grad_w


def solution(mesh):
    tokens = P("dp", "seq", "tensor")
    in_specs = (tokens, tokens, tokens, P("dp", "tensor", None), P("tensor", None), tokens)
    out_specs = (tokens, tokens, tokens, P(("dp", "seq"), "tensor"))

    step = jax.shard_map(local, mesh=mesh, in_specs=in_specs, out_specs=out_specs, check_vma=False)
    if not paired_mesh(*(mesh.shape[axis] for axis in ("dp", "seq", "tensor"))):
        return step

    return step
```

```python
import functools
import math

import jax
import jax.numpy as jnp
from jax import lax
from jax.experimental import pallas as pl
from jax.experimental.pallas import tpu as pltpu
from jax.sharding import PartitionSpec as P


F32 = jnp.float32
BF16 = jnp.bfloat16
TILE = 256
GRANT = 24 * 1024 * 1024


def dot_nn(a, b):
    return lax.dot_general(a, b, (((1,), (0,)), ((), ())), preferred_element_type=F32)


def dot_nt(a, b):
    return lax.dot_general(a, b, (((1,), (1,)), ((), ())), preferred_element_type=F32)


def dot_tn(a, b):
    return lax.dot_general(a, b, (((0,), (0,)), ((), ())), preferred_element_type=F32)


def call(body, outs, args, scalars=None, scratch=(), near=True):
    count = 0 if scalars is None else 1
    whole = pl.BlockSpec(memory_space=pltpu.VMEM)
    given = whole if near else pl.BlockSpec(memory_space=pltpu.HBM)
    spec = pltpu.PrefetchScalarGridSpec(
        num_scalar_prefetch=count,
        in_specs=[given] * len(args),
        out_specs=[whole] * len(outs),
        scratch_shapes=list(scratch),
    )
    prefix = () if scalars is None else (scalars,)
    args = [pltpu.with_memory_space_constraint(x, pltpu.VMEM if near else pltpu.HBM) for x in args]
    limit = pltpu.CompilerParams(vmem_limit_bytes=GRANT)
    return pl.pallas_call(body, out_shape=list(outs), grid_spec=spec, compiler_params=limit)(*prefix, *args)


def after(value, *others):
    return lax.optimization_barrier((value, *others))[0]


def shape(dims, kind):
    return pltpu.VMEM(dims, kind)


def final(dims, kind):
    return jax.ShapeDtypeStruct(dims, kind)


def running_sum(values):
    length = values.shape[1]
    position = lax.broadcasted_iota(jnp.int32, values.shape, 1)
    step = 1
    while step < length:
        values = values + jnp.where(position >= step, pltpu.roll(values, step, 1), 0.0)
        step *= 2
    return values


def span_decay(decay_ref, start, stop):
    values = decay_ref[...]
    position = lax.broadcasted_iota(jnp.int32, values.shape, 1)
    inside = (position >= start) & (position < stop)
    return jnp.exp(jnp.sum(jnp.where(inside, values, 0.0), axis=1, keepdims=True))


def states_kernel(place, decay_in, query_in, key_in, value_in, *refs, heads):
    *outs, semaphores = refs
    state_ref, row_ref, column_ref, decay_ref, query_ref, key_ref, value_ref = outs
    rows = key_ref.shape[0]
    width = key_ref.shape[1] // heads
    spans = [slice(h * width, (h + 1) * width) for h in range(heads)]
    pairs = ((decay_in, decay_ref), (key_in, key_ref), (value_in, value_ref), (query_in, query_ref))
    copies = [pltpu.make_async_copy(*pair, semaphores.at[n]) for n, pair in enumerate(pairs)]
    for copy in copies:
        copy.start()
    copies[0].wait()
    local = decay_ref[:, pl.ds(pl.multiple_of(place[0] * rows, 128), rows)]
    tall = row_ref.shape[0]
    local = jnp.concatenate([local] * pl.cdiv(tall, heads), axis=0)[:tall]
    cumulative = running_sum(local)
    columns = cumulative.T
    row_ref[...] = cumulative
    column_ref[...] = columns
    copies[1].wait()
    copies[2].wait()
    for h, at in enumerate(spans):
        to_end = jnp.exp(cumulative[h : h + 1, rows - 1 : rows] - columns[:, h : h + 1])
        scaled = (key_ref[:, at].astype(F32) * to_end).astype(BF16)
        state_ref[h] = dot_tn(scaled, value_ref[:, at]).astype(BF16)
    copies[3].wait()


def tiles(rows):
    return [(i, j) for i in range(rows // TILE) for j in range(i + 1)]


def tile_decay(row_ref, column_ref, h, i, j):
    spread = column_ref[i * TILE : (i + 1) * TILE, h : h + 1] - row_ref[h : h + 1, j * TILE : (j + 1) * TILE]
    if i != j:
        return jnp.exp(spread)
    later = lax.broadcasted_iota(jnp.int32, (TILE, TILE), 0)
    earlier = lax.broadcasted_iota(jnp.int32, (TILE, TILE), 1)
    lower = later >= earlier
    return jnp.where(lower, jnp.exp(jnp.where(lower, spread, 0.0)), 0.0)


def weights_kernel(query_ref, key_ref, value_ref, row_ref, column_ref, weight_ref, within_ref, *, heads):
    rows = key_ref.shape[0]
    width = key_ref.shape[1] // heads
    for h in range(heads):
        at = slice(h * width, (h + 1) * width)
        sums = {}
        for n, (i, j) in enumerate(tiles(rows)):
            ti, tj = slice(i * TILE, (i + 1) * TILE), slice(j * TILE, (j + 1) * TILE)
            scores = dot_nt(query_ref[ti, at], key_ref[tj, at])
            weight = (scores * tile_decay(row_ref, column_ref, h, i, j) * (1.0 / width)).astype(BF16)
            weight_ref[h, n] = weight
            term = dot_nn(weight, value_ref[tj, at])
            sums[i] = term if i not in sums else sums[i] + term
        for i, total in sums.items():
            within_ref[i * TILE : (i + 1) * TILE, at] = total


def gather_states(decay_ref, pieces, place, rows, forward):
    factors = []
    for k in range(2, len(pieces) + 1):
        start = (place - k + 1) * rows if forward else (place + 1) * rows
        stop = place * rows if forward else (place + k) * rows
        factors.append(span_decay(decay_ref, start, stop))

    def state(h):
        total = pieces[0][h].astype(F32)
        for factor, piece in zip(factors, pieces[1:], strict=True):
            total = total + factor[h : h + 1] * piece[h].astype(F32)
        return total.astype(BF16)

    return state


def attend(place, decay_ref, query_ref, within_ref, column_ref, pieces, attn_ref, carried_ref, heads):
    rows = query_ref.shape[0]
    width = query_ref.shape[1] // heads
    state = gather_states(decay_ref, pieces, place[0], rows, True)
    for h in range(heads):
        at = slice(h * width, (h + 1) * width)
        carried = state(h)
        carried_ref[h] = carried
        scaled = query_ref[:, at].astype(F32) * (jnp.exp(column_ref[:, h : h + 1]) * (1.0 / width))
        attn_ref[:, at] = (within_ref[:, at] + dot_nn(scaled.astype(BF16), carried)).astype(BF16)


def project(place, grad_ref, attn_ref, send_ref, keep_ref, scale):
    half = keep_ref.shape[0]
    for core, into in ((1 - place[1], send_ref), (place[1], keep_ref)):
        at = pl.ds(pl.multiple_of(core * half, 128), half)
        into[...] = (dot_tn(grad_ref[:, at], attn_ref[...]) * scale).astype(BF16)


def attention_kernel(place, decay_ref, query_ref, within_ref, column_ref, *refs, heads):
    *pieces, attn_ref, carried_ref = refs
    attend(place, decay_ref, query_ref, within_ref, column_ref, pieces, attn_ref, carried_ref, heads)


def attention_project_kernel(place, decay_ref, query_ref, within_ref, column_ref, grad_ref, *refs, heads, scale):
    *pieces, attn_ref, carried_ref, send_ref, keep_ref = refs
    attend(place, decay_ref, query_ref, within_ref, column_ref, pieces, attn_ref, carried_ref, heads)
    project(place, grad_ref, attn_ref, send_ref, keep_ref, scale)


def projection_kernel(place, grad_ref, attn_ref, send_ref, keep_ref, *, scale):
    project(place, grad_ref, attn_ref, send_ref, keep_ref, scale)


def half_columns(out_ref, index, count):
    return out_ref[:, pl.ds(pl.multiple_of(index * count, 128), count)]


def grad_attn_half_kernel(place, grad_ref, out_ref, total_ref):
    total_ref[...] = dot_nt(grad_ref[...], half_columns(out_ref, place[3], grad_ref.shape[1]))


def grad_attn_kernel(place, grad_ref, out_ref, query_ref, column_ref, *refs, heads):
    *halves, grad_attn_ref, back_ref = refs
    width = query_ref.shape[1] // heads
    if halves:
        total = halves[0][...] + dot_nt(grad_ref[...], half_columns(out_ref, 1 - place[3], grad_ref.shape[1]))
    else:
        total = dot_nt(grad_ref[...], out_ref[...])
    total = total.astype(BF16)
    grad_attn_ref[...] = total
    for h in range(heads):
        at = slice(h * width, (h + 1) * width)
        scaled = query_ref[:, at].astype(F32) * (jnp.exp(column_ref[:, h : h + 1]) * (1.0 / width))
        back_ref[h] = dot_tn(scaled.astype(BF16), total[:, at]).astype(BF16)


def chain_kernel(place, decay_ref, back_ref, came_ref, chain_ref, *, rows):
    factor = span_decay(decay_ref, place[0] * rows, (place[0] + 1) * rows)
    for h in range(back_ref.shape[0]):
        chain_ref[h] = (back_ref[h].astype(F32) + factor[h : h + 1] * came_ref[h].astype(F32)).astype(BF16)


def inner_kernel(
    query_ref, key_ref, value_ref, grad_ref, row_ref, column_ref, weight_ref, carried_ref, dq_ref, dk_ref, dv_ref, *, heads
):
    rows = key_ref.shape[0]
    width = key_ref.shape[1] // heads
    inverse = 1.0 / width
    for h in range(heads):
        at = slice(h * width, (h + 1) * width)
        dq, dk, dv = {}, {}, {}

        def add(store, index, term):
            store[index] = term if index not in store else store[index] + term

        for n, (i, j) in enumerate(tiles(rows)):
            ti, tj = slice(i * TILE, (i + 1) * TILE), slice(j * TILE, (j + 1) * TILE)
            scores = dot_nt(grad_ref[ti, at], value_ref[tj, at])
            weight = (scores * tile_decay(row_ref, column_ref, h, i, j) * inverse).astype(BF16)
            add(dq, i, dot_nn(weight, key_ref[tj, at]))
            add(dk, j, dot_tn(weight, query_ref[ti, at]))
            add(dv, j, dot_tn(weight_ref[h, n], grad_ref[ti, at]))
        for i in range(rows // TILE):
            ti = slice(i * TILE, (i + 1) * TILE)
            scaled = grad_ref[ti, at].astype(F32) * (jnp.exp(column_ref[ti, h : h + 1]) * inverse)
            dq_ref[ti, at] = (dq[i] + dot_nt(scaled.astype(BF16), carried_ref[h])).astype(BF16)
            dk_ref[ti, at] = dk[i]
            dv_ref[ti, at] = dv[i]


def summed_states(pieces):
    def state(h):
        total = pieces[0][h]
        for piece in pieces[1:]:
            total = total + piece[h]
        return total

    return state


def outer_kernel(place, decay_ref, key_ref, value_ref, row_ref, column_ref, inner_k_ref, inner_v_ref, *refs, heads, chained):
    *pieces, dk_ref, dv_ref = refs
    rows = key_ref.shape[0]
    width = key_ref.shape[1] // heads
    state = summed_states(pieces) if chained else gather_states(decay_ref, pieces, place[0], rows, False)
    for h in range(heads):
        at = slice(h * width, (h + 1) * width)
        back = state(h)
        to_end = jnp.exp(row_ref[h : h + 1, rows - 1 : rows] - column_ref[:, h : h + 1])
        values = (value_ref[:, at].astype(F32) * to_end).astype(BF16)
        keys = (key_ref[:, at].astype(F32) * to_end).astype(BF16)
        dk_ref[:, at] = (inner_k_ref[:, at] + dot_nt(values, back)).astype(BF16)
        dv_ref[:, at] = (inner_v_ref[:, at] + dot_nn(keys, back)).astype(BF16)


def pieces_kernel(place, mine_ref, other_ref, keep_ref, send_ref):
    rows = keep_ref.shape[1]
    for n in range(4):
        owner = place[0] ^ (2, 0, 3, 1)[n]
        at = pl.ds(pl.multiple_of(owner * rows, 16), rows)
        total = mine_ref[at, :].astype(F32) + other_ref[at, :].astype(F32)
        if n < 2:
            keep_ref[n] = total
        else:
            send_ref[n - 2] = total.astype(BF16)


def direct_kernel(place, mine_ref, other_ref, keep_ref, *send_refs):
    count, rows = len(send_refs) + 1, keep_ref.shape[0]
    for k in range(count):
        at = pl.ds(pl.multiple_of(lax.rem(place[0] + k, count) * rows, 16), rows)
        total = mine_ref[at, :].astype(F32) + other_ref[at, :].astype(F32)
        if k == 0:
            keep_ref[...] = total
        else:
            send_refs[k - 1][...] = total.astype(BF16)


def halve_kernel(mine_ref, other_ref, keep_ref, send_ref):
    send_ref[...] = (mine_ref[0] + other_ref[0].astype(F32)).astype(BF16)
    keep_ref[...] = mine_ref[1] + other_ref[1].astype(F32)


def finish_kernel(place, *refs):
    own_ref, *own_others, far_ref, far_other_ref, keep_ref, send_ref = refs
    own = own_ref[...]
    for ref in own_others:
        own = own + ref[...].astype(F32)
    far = far_ref[...] + far_other_ref[...].astype(F32)
    mine = place[2] == place[3]
    send_ref[...] = jnp.where(mine, far, own).astype(BF16)
    keep_ref[...] = jnp.where(mine, own, far)


def shift_up(value, count):
    return [lax.ppermute(value, "seq", [(i, i + k) for i in range(count - k)]) for k in range(1, count)]


def shift_down(value, count):
    return [lax.ppermute(value, "seq", [(i, i - k) for i in range(k, count)]) for k in range(1, count)]


def swap(value, axis, bit):
    return lax.ppermute(value, axis, [(i, i ^ bit) for i in range(lax.axis_size(axis))])


def paired_mesh(dp_count, seq_count, tensor_count):
    return tensor_count == 2 and dp_count == 2 * tensor_count and seq_count == 4


def local(queries, key_vectors, value_vectors, log_decay, w_out, grad_out):
    micro, rows, features = queries.shape
    heads = log_decay.shape[1]
    width = features // heads
    dp_count, seq_count, tensor_count = (lax.axis_size(n) for n in ("dp", "seq", "tensor"))
    seq_index, dp_index, tensor_index = (lax.axis_index(n) for n in ("seq", "dp", "tensor"))
    scale = 1.0 / math.sqrt(micro * dp_count * rows * seq_count)
    query, key, value = queries[0], key_vectors[0], value_vectors[0]
    decay, grad = log_decay[0], grad_out[0]
    columns = grad.shape[1]
    paired = paired_mesh(dp_count, seq_count, tensor_count)
    place = jnp.stack([seq_index, dp_index % 2, dp_index // 2, tensor_index]).astype(jnp.int32)
    tall = -(-heads // 8) * 8
    state_shape = shape((heads, width, width), BF16)
    token_f32, token_bf16 = shape((rows, features), F32), shape((rows, features), BF16)

    if paired:
        other = swap(grad, "tensor", 1)
    else:
        other = lax.all_gather(grad, "tensor", axis=1, tiled=True)

    state, row, column, decay, query, key, value = call(
        functools.partial(states_kernel, heads=heads),
        [state_shape, shape((tall, rows), F32), shape((rows, tall), F32), shape(decay.shape, F32)] + [token_bf16] * 3,
        [decay, query, key, value],
        place,
        [pltpu.SemaphoreType.DMA((4,))],
        near=False,
    )
    received = shift_up(state, seq_count)
    weight, within = call(
        functools.partial(weights_kernel, heads=heads),
        [shape((heads, len(tiles(rows)), TILE, TILE), BF16), token_f32],
        [query, key, value, row, column],
    )
    attend_args = [decay, query, within, column]

    if paired:
        dest = columns // 2
        piece = dest // seq_count
        parts = [shape((dest, features), BF16)] * 2

        quarter = (piece, features)

        def spread(send, keep, *behind):
            came = swap(send, "dp", 1)
            stay, go = call(
                pieces_kernel,
                [shape((2, *quarter), F32), shape((2, *quarter), BF16)],
                [after(keep, *behind), came],
                place,
            )
            return stay, swap(go, "seq", 1)

        def halve(stay, came, *behind):
            stay, go = call(halve_kernel, [shape(quarter, F32), shape(quarter, BF16)], [after(stay, *behind), came])
            return stay, swap(go, "seq", 2)

        attn, carried, send, keep = call(
            functools.partial(attention_project_kernel, heads=heads, scale=scale),
            [token_bf16, state_shape, *parts],
            [*attend_args, grad, *received],
            place,
        )
        came = swap(send, "dp", 1)
        own_stay, *own_parts = call(
            direct_kernel,
            [shape(quarter, F32)] + [shape(quarter, BF16)] * (seq_count - 1),
            [keep, came],
            place,
        )
        own_came = [
            lax.ppermute(part, "seq", [(i, (i + k) % seq_count) for i in range(seq_count)])
            for k, part in enumerate(own_parts, 1)
        ]
        (half,) = call(grad_attn_half_kernel, [token_f32], [grad, after(w_out, own_stay)], place)
        send, keep_far = call(
            functools.partial(projection_kernel, scale=scale), parts, [other, after(attn, half)], place
        )
        last = (half,)
    else:
        attn, carried = call(
            functools.partial(attention_kernel, heads=heads),
            [token_bf16, state_shape],
            [*attend_args, *received],
            place,
        )
        partial = (dot_tn(other, attn) * scale).astype(BF16)
        grad_w = lax.psum_scatter(partial, ("dp", "seq"), scatter_dimension=0, tiled=True).astype(F32)
        last, keep = (), attn

    if paired:
        keep = keep_far
    grad_attn, back = call(
        functools.partial(grad_attn_kernel, heads=heads),
        [token_bf16, state_shape],
        [other, w_out, after(query, keep), column, *last],
        place,
    )

    def pass_back(value, stage):
        return lax.ppermute(value, "seq", [(seq_count - stage, seq_count - 1 - stage)])

    returned = [pass_back(back, 1)] if paired else shift_down(back, seq_count)
    if paired:
        far_stay, far_came = spread(send, keep_far, back)
        grad_attn = after(grad_attn, far_stay)
    grad_queries, inner_keys, inner_values = call(
        functools.partial(inner_kernel, heads=heads),
        [final((rows, features), BF16), token_f32, token_f32],
        [query, key, value, grad_attn, row, column, weight, carried],
    )
    if paired:
        def chain(stage, *behind):
            (passed,) = call(
                functools.partial(chain_kernel, rows=rows),
                [state_shape],
                [decay, after(back, *behind), returned[-1]],
                place,
            )
            return pass_back(passed, stage)

        returned.append(chain(2, inner_keys))
        far_stay, far_came = halve(far_stay, far_came, inner_keys)
        returned.append(chain(3, far_stay))
        keep, send = call(
            finish_kernel,
            [shape(quarter, F32), shape(quarter, BF16)],
            [own_stay, *own_came, far_stay, far_came],
            place,
        )
        crossed = swap(send, "dp", 2)
        inner_keys = after(inner_keys, keep)
    grad_keys, grad_values = call(
        functools.partial(outer_kernel, heads=heads, chained=paired),
        [final((rows, features), BF16)] * 2,
        [decay, key, value, row, column, inner_keys, inner_values, *returned],
        place,
    )
    if paired:
        grad_w = keep + crossed.astype(F32)
    return grad_queries[None], grad_keys[None], grad_values[None], grad_w


def solution(mesh):
    tokens = P("dp", "seq", "tensor")
    in_specs = (tokens, tokens, tokens, P("dp", "tensor", None), P("tensor", None), tokens)
    out_specs = (tokens, tokens, tokens, P(("dp", "seq"), "tensor"))

    step = jax.shard_map(local, mesh=mesh, in_specs=in_specs, out_specs=out_specs, check_vma=False)
    if not paired_mesh(*(mesh.shape[axis] for axis in ("dp", "seq", "tensor"))):
        return step

    return step
```

```python
import functools
import math

import jax
import jax.numpy as jnp
from jax import lax
from jax.experimental import pallas as pl
from jax.experimental.pallas import tpu as pltpu
from jax.sharding import PartitionSpec as P


F32 = jnp.float32
BF16 = jnp.bfloat16
TILE = 256
FIRST = 256
GRANT = 24 * 1024 * 1024


def dot_nn(a, b):
    return lax.dot_general(a, b, (((1,), (0,)), ((), ())), preferred_element_type=F32)


def dot_nt(a, b):
    return lax.dot_general(a, b, (((1,), (1,)), ((), ())), preferred_element_type=F32)


def dot_tn(a, b):
    return lax.dot_general(a, b, (((0,), (0,)), ((), ())), preferred_element_type=F32)


def call(body, outs, args, scalars=None, scratch=(), near=True):
    count = 0 if scalars is None else 1
    whole = pl.BlockSpec(memory_space=pltpu.VMEM)
    given = whole if near else pl.BlockSpec(memory_space=pltpu.HBM)
    spec = pltpu.PrefetchScalarGridSpec(
        num_scalar_prefetch=count,
        in_specs=[given] * len(args),
        out_specs=[whole] * len(outs),
        scratch_shapes=list(scratch),
    )
    prefix = () if scalars is None else (scalars,)
    args = [pltpu.with_memory_space_constraint(x, pltpu.VMEM if near else pltpu.HBM) for x in args]
    limit = pltpu.CompilerParams(vmem_limit_bytes=GRANT)
    return pl.pallas_call(body, out_shape=list(outs), grid_spec=spec, compiler_params=limit)(*prefix, *args)


def after(value, *others):
    return lax.optimization_barrier((value, *others))[0]


def shape(dims, kind):
    return pltpu.VMEM(dims, kind)


def final(dims, kind):
    return jax.ShapeDtypeStruct(dims, kind)


def running_sum(values):
    length = values.shape[1]
    position = lax.broadcasted_iota(jnp.int32, values.shape, 1)
    step = 1
    while step < length:
        values = values + jnp.where(position >= step, pltpu.roll(values, step, 1), 0.0)
        step *= 2
    return values


def span_decay(decay_ref, start, stop):
    values = decay_ref[...]
    position = lax.broadcasted_iota(jnp.int32, values.shape, 1)
    inside = (position >= start) & (position < stop)
    return jnp.exp(jnp.sum(jnp.where(inside, values, 0.0), axis=1, keepdims=True))


def states_kernel(place, decay_in, query_in, key_in, value_in, *refs, heads):
    *outs, semaphores = refs
    state_ref, row_ref, column_ref, decay_ref, query_ref, key_ref, value_ref = outs
    rows = key_ref.shape[0]
    width = key_ref.shape[1] // heads
    spans = [slice(h * width, (h + 1) * width) for h in range(heads)]
    pairs = ((decay_in, decay_ref), (key_in, key_ref), (value_in, value_ref), (query_in, query_ref))
    copies = [pltpu.make_async_copy(*pair, semaphores.at[n]) for n, pair in enumerate(pairs)]
    for copy in copies:
        copy.start()
    copies[0].wait()
    local = decay_ref[:, pl.ds(pl.multiple_of(place[0] * rows, 128), rows)]
    tall = row_ref.shape[0]
    local = jnp.concatenate([local] * pl.cdiv(tall, heads), axis=0)[:tall]
    cumulative = running_sum(local)
    columns = cumulative.T
    row_ref[...] = cumulative
    column_ref[...] = columns
    copies[1].wait()
    copies[2].wait()
    for h, at in enumerate(spans):
        to_end = jnp.exp(cumulative[h : h + 1, rows - 1 : rows] - columns[:, h : h + 1])
        scaled = (key_ref[:, at].astype(F32) * to_end).astype(BF16)
        state_ref[h] = dot_tn(scaled, value_ref[:, at]).astype(BF16)
    copies[3].wait()


def tiles(rows):
    return [(i, j) for i in range(rows // TILE) for j in range(i + 1)]


def tile_decay(row_ref, column_ref, h, i, j):
    spread = column_ref[i * TILE : (i + 1) * TILE, h : h + 1] - row_ref[h : h + 1, j * TILE : (j + 1) * TILE]
    if i != j:
        return jnp.exp(spread)
    later = lax.broadcasted_iota(jnp.int32, (TILE, TILE), 0)
    earlier = lax.broadcasted_iota(jnp.int32, (TILE, TILE), 1)
    lower = later >= earlier
    return jnp.where(lower, jnp.exp(jnp.where(lower, spread, 0.0)), 0.0)


def weights_kernel(query_ref, key_ref, value_ref, row_ref, column_ref, weight_ref, within_ref, *, heads):
    rows = key_ref.shape[0]
    width = key_ref.shape[1] // heads
    for h in range(heads):
        at = slice(h * width, (h + 1) * width)
        sums = {}
        for n, (i, j) in enumerate(tiles(rows)):
            ti, tj = slice(i * TILE, (i + 1) * TILE), slice(j * TILE, (j + 1) * TILE)
            scores = dot_nt(query_ref[ti, at], key_ref[tj, at])
            weight = (scores * tile_decay(row_ref, column_ref, h, i, j) * (1.0 / width)).astype(BF16)
            weight_ref[h, n] = weight
            term = dot_nn(weight, value_ref[tj, at])
            sums[i] = term if i not in sums else sums[i] + term
        for i, total in sums.items():
            within_ref[i * TILE : (i + 1) * TILE, at] = total


def gather_states(decay_ref, pieces, place, rows, forward):
    factors = []
    for k in range(2, len(pieces) + 1):
        start = (place - k + 1) * rows if forward else (place + 1) * rows
        stop = place * rows if forward else (place + k) * rows
        factors.append(span_decay(decay_ref, start, stop))

    def state(h):
        total = pieces[0][h].astype(F32)
        for factor, piece in zip(factors, pieces[1:], strict=True):
            total = total + factor[h : h + 1] * piece[h].astype(F32)
        return total.astype(BF16)

    return state


def attend(place, decay_ref, query_ref, within_ref, column_ref, pieces, attn_ref, carried_ref, heads):
    rows = query_ref.shape[0]
    width = query_ref.shape[1] // heads
    state = gather_states(decay_ref, pieces, place[0], rows, True)
    for h in range(heads):
        at = slice(h * width, (h + 1) * width)
        carried = state(h)
        carried_ref[h] = carried
        scaled = query_ref[:, at].astype(F32) * (jnp.exp(column_ref[:, h : h + 1]) * (1.0 / width))
        attn_ref[:, at] = (within_ref[:, at] + dot_nn(scaled.astype(BF16), carried)).astype(BF16)


def project(place, grad_ref, attn_ref, send_ref, keep_ref, scale, start=0):
    half, wide = keep_ref.shape
    attn = attn_ref[:, start : start + wide]
    for core, into in ((1 - place[1], send_ref), (place[1], keep_ref)):
        at = pl.ds(pl.multiple_of(core * half, 128), half)
        into[...] = (dot_tn(grad_ref[:, at], attn) * scale).astype(BF16)


def attention_kernel(place, decay_ref, query_ref, within_ref, column_ref, *refs, heads):
    *pieces, attn_ref, carried_ref = refs
    attend(place, decay_ref, query_ref, within_ref, column_ref, pieces, attn_ref, carried_ref, heads)


def attention_project_kernel(place, decay_ref, query_ref, within_ref, column_ref, grad_ref, *refs, heads, scale):
    *pieces, attn_ref, carried_ref, send_ref, keep_ref = refs
    attend(place, decay_ref, query_ref, within_ref, column_ref, pieces, attn_ref, carried_ref, heads)
    project(place, grad_ref, attn_ref, send_ref, keep_ref, scale)


def projection_kernel(place, grad_ref, attn_ref, send_ref, keep_ref, *, scale, start):
    project(place, grad_ref, attn_ref, send_ref, keep_ref, scale, start)


def half_columns(out_ref, index, count):
    return out_ref[:, pl.ds(pl.multiple_of(index * count, 128), count)]


def grad_attn_half_kernel(place, grad_ref, out_ref, total_ref):
    total_ref[...] = dot_nt(grad_ref[...], half_columns(out_ref, place[3], grad_ref.shape[1]))


def grad_attn_kernel(place, grad_ref, out_ref, query_ref, column_ref, *refs, heads):
    *halves, grad_attn_ref, back_ref = refs
    width = query_ref.shape[1] // heads
    if halves:
        total = halves[0][...] + dot_nt(grad_ref[...], half_columns(out_ref, 1 - place[3], grad_ref.shape[1]))
    else:
        total = dot_nt(grad_ref[...], out_ref[...])
    total = total.astype(BF16)
    grad_attn_ref[...] = total
    for h in range(heads):
        at = slice(h * width, (h + 1) * width)
        scaled = query_ref[:, at].astype(F32) * (jnp.exp(column_ref[:, h : h + 1]) * (1.0 / width))
        back_ref[h] = dot_tn(scaled.astype(BF16), total[:, at]).astype(BF16)


def chain_kernel(place, decay_ref, back_ref, came_ref, chain_ref, *, rows):
    factor = span_decay(decay_ref, place[0] * rows, (place[0] + 1) * rows)
    for h in range(back_ref.shape[0]):
        chain_ref[h] = (back_ref[h].astype(F32) + factor[h : h + 1] * came_ref[h].astype(F32)).astype(BF16)


def inner_kernel(
    query_ref, key_ref, value_ref, grad_ref, row_ref, column_ref, weight_ref, carried_ref, dq_ref, dk_ref, dv_ref, *, heads
):
    rows = key_ref.shape[0]
    width = key_ref.shape[1] // heads
    inverse = 1.0 / width
    for h in range(heads):
        at = slice(h * width, (h + 1) * width)
        dq, dk, dv = {}, {}, {}

        def add(store, index, term):
            store[index] = term if index not in store else store[index] + term

        for n, (i, j) in enumerate(tiles(rows)):
            ti, tj = slice(i * TILE, (i + 1) * TILE), slice(j * TILE, (j + 1) * TILE)
            scores = dot_nt(grad_ref[ti, at], value_ref[tj, at])
            weight = (scores * tile_decay(row_ref, column_ref, h, i, j) * inverse).astype(BF16)
            add(dq, i, dot_nn(weight, key_ref[tj, at]))
            add(dk, j, dot_tn(weight, query_ref[ti, at]))
            add(dv, j, dot_tn(weight_ref[h, n], grad_ref[ti, at]))
        for i in range(rows // TILE):
            ti = slice(i * TILE, (i + 1) * TILE)
            scaled = grad_ref[ti, at].astype(F32) * (jnp.exp(column_ref[ti, h : h + 1]) * inverse)
            dq_ref[ti, at] = (dq[i] + dot_nt(scaled.astype(BF16), carried_ref[h])).astype(BF16)
            dk_ref[ti, at] = dk[i]
            dv_ref[ti, at] = dv[i]


def summed_states(pieces):
    def state(h):
        total = pieces[0][h]
        for piece in pieces[1:]:
            total = total + piece[h]
        return total

    return state


def outer_kernel(place, decay_ref, key_ref, value_ref, row_ref, column_ref, inner_k_ref, inner_v_ref, *refs, heads, chained):
    *pieces, dk_ref, dv_ref = refs
    rows = key_ref.shape[0]
    width = key_ref.shape[1] // heads
    state = summed_states(pieces) if chained else gather_states(decay_ref, pieces, place[0], rows, False)
    for h in range(heads):
        at = slice(h * width, (h + 1) * width)
        back = state(h)
        to_end = jnp.exp(row_ref[h : h + 1, rows - 1 : rows] - column_ref[:, h : h + 1])
        values = (value_ref[:, at].astype(F32) * to_end).astype(BF16)
        keys = (key_ref[:, at].astype(F32) * to_end).astype(BF16)
        dk_ref[:, at] = (inner_k_ref[:, at] + dot_nt(values, back)).astype(BF16)
        dv_ref[:, at] = (inner_v_ref[:, at] + dot_nn(keys, back)).astype(BF16)


def owner_turns(bit):
    return (3 - bit, 0, 3, bit)


def sum_kernel(mine_ref, other_ref, keep_ref, send_ref):
    total = mine_ref[...].astype(F32) + other_ref[...].astype(F32)
    keep_ref[...] = total
    send_ref[...] = total.astype(BF16)


def pieces_kernel(place, mine_ref, other_ref, keep_ref, send_ref):
    rows = keep_ref.shape[1]
    for n, turn in enumerate(owner_turns(1)):
        at = pl.ds(pl.multiple_of((place[0] ^ turn) * rows, 16), rows)
        total = mine_ref[at, :].astype(F32) + other_ref[at, :].astype(F32)
        if n < 2:
            keep_ref[n] = total
        else:
            send_ref[n - 2] = total.astype(BF16)


def own_kernel(place, mine_ref, other_ref, keep_ref, send_ref, later_keep_ref, later_send_ref):
    _, rows, wide = keep_ref.shape
    for n, turn in enumerate(owner_turns(1)):
        at = pl.ds(pl.multiple_of((place[0] ^ turn) * rows, 16), rows)
        total = mine_ref[at, :wide].astype(F32) + other_ref[at, :wide].astype(F32)
        if n < 2:
            keep_ref[n] = total
        else:
            send_ref[n - 2] = total.astype(BF16)
    later = mine_ref[:, wide:].astype(F32) + other_ref[:, wide:].astype(F32)
    later_keep_ref[...] = later
    later_send_ref[...] = later.astype(BF16)


def later_kernel(place, own_ref, own_other_ref, far_ref, far_other_ref, keep_ref, send_ref):
    rows = keep_ref.shape[1]
    mine = place[2] == place[3]
    for n, turn in enumerate(owner_turns(1)):
        at = pl.ds(pl.multiple_of((place[0] ^ turn) * rows, 16), rows)
        kept = jnp.where(mine, own_ref[at, :], far_ref[at, :])
        came = jnp.where(mine, own_other_ref[at, :].astype(F32), far_other_ref[at, :].astype(F32))
        if n < 2:
            keep_ref[n] = kept + came
        else:
            send_ref[n - 2] = (kept + came).astype(BF16)


def halve_kernel(mine_ref, other_ref, keep_ref, send_ref):
    send_ref[...] = (mine_ref[0] + other_ref[0].astype(F32)).astype(BF16)
    keep_ref[...] = mine_ref[1] + other_ref[1].astype(F32)


def finish_kernel(place, own_ref, own_other_ref, far_ref, far_other_ref, keep_ref, send_ref):
    own = own_ref[...] + own_other_ref[...].astype(F32)
    far = far_ref[...] + far_other_ref[...].astype(F32)
    mine = place[2] == place[3]
    send_ref[...] = jnp.where(mine, far, own).astype(BF16)
    keep_ref[...] = jnp.where(mine, own, far)


def result_kernel(first_ref, crossed_ref, later_ref, later_other_ref, out_ref):
    wide = first_ref.shape[1]
    out_ref[:, :wide] = first_ref[...] + crossed_ref[...].astype(F32)
    out_ref[:, wide:] = later_ref[...] + later_other_ref[...].astype(F32)


def shift_up(value, count):
    return [lax.ppermute(value, "seq", [(i, i + k) for i in range(count - k)]) for k in range(1, count)]


def shift_down(value, count):
    return [lax.ppermute(value, "seq", [(i, i - k) for i in range(k, count)]) for k in range(1, count)]


def to_chip(value, own):
    tensor_count = lax.axis_size("tensor")
    pairs = []
    for t in range(tensor_count):
        target = t if own else 1 - t
        for core in range(2):
            start = (2 * (1 - target) + core) * tensor_count + t
            pairs.append((start, (2 * target + core) * tensor_count + t))
    return lax.ppermute(value, ("dp", "tensor"), pairs)


def swap(value, axis, bit):
    return lax.ppermute(value, axis, [(i, i ^ bit) for i in range(lax.axis_size(axis))])


def paired_mesh(dp_count, seq_count, tensor_count):
    return tensor_count == 2 and dp_count == 2 * tensor_count and seq_count == 4


def local(queries, key_vectors, value_vectors, log_decay, w_out, grad_out):
    micro, rows, features = queries.shape
    heads = log_decay.shape[1]
    width = features // heads
    dp_count, seq_count, tensor_count = (lax.axis_size(n) for n in ("dp", "seq", "tensor"))
    seq_index, dp_index, tensor_index = (lax.axis_index(n) for n in ("seq", "dp", "tensor"))
    scale = 1.0 / math.sqrt(micro * dp_count * rows * seq_count)
    query, key, value = queries[0], key_vectors[0], value_vectors[0]
    decay, grad = log_decay[0], grad_out[0]
    columns = grad.shape[1]
    paired = paired_mesh(dp_count, seq_count, tensor_count)
    place = jnp.stack([seq_index, dp_index % 2, dp_index // 2, tensor_index]).astype(jnp.int32)
    tall = -(-heads // 8) * 8
    state_shape = shape((heads, width, width), BF16)
    token_f32, token_bf16 = shape((rows, features), F32), shape((rows, features), BF16)

    if paired:
        other = swap(grad, "tensor", 1)
    else:
        other = lax.all_gather(grad, "tensor", axis=1, tiled=True)

    state, row, column, decay, query, key, value = call(
        functools.partial(states_kernel, heads=heads),
        [state_shape, shape((tall, rows), F32), shape((rows, tall), F32), shape(decay.shape, F32)] + [token_bf16] * 3,
        [decay, query, key, value],
        place,
        [pltpu.SemaphoreType.DMA((4,))],
        near=False,
    )
    received = shift_up(state, seq_count)
    weight, within = call(
        functools.partial(weights_kernel, heads=heads),
        [shape((heads, len(tiles(rows)), TILE, TILE), BF16), token_f32],
        [query, key, value, row, column],
    )
    attend_args = [decay, query, within, column]

    if paired:
        dest = columns // 2
        piece = dest // seq_count
        parts = [shape((dest, features), BF16)] * 2

        quarter = (piece, features)

        first_part, later_part = (piece, FIRST), (piece, features - FIRST)

        def halve(stay, came, *behind):
            dims = stay.shape[1:]
            return call(halve_kernel, [shape(dims, F32), shape(dims, BF16)], [after(stay, *behind), came])

        attn, carried, send, keep = call(
            functools.partial(attention_project_kernel, heads=heads, scale=scale),
            [token_bf16, state_shape, *parts],
            [*attend_args, grad, *received],
            place,
        )
        own_swap = swap(send, "dp", 1)
        own_stay, go, own_later, later_go = call(
            own_kernel,
            [
                shape((2, *first_part), F32),
                shape((2, *first_part), BF16),
                shape((dest, features - FIRST), F32),
                shape((dest, features - FIRST), BF16),
            ],
            [keep, own_swap],
            place,
        )
        own_came = swap(go, "seq", 1)
        own_later_came = to_chip(later_go, True)
        (half,) = call(grad_attn_half_kernel, [token_f32], [grad, after(w_out, own_stay)], place)

        own_stay, go = halve(own_stay, own_came, half)
        own_came = swap(go, "seq", 2)

        def project_far(start, width, *behind):
            send, keep = call(
                functools.partial(projection_kernel, scale=scale, start=start),
                [shape((dest, width), BF16)] * 2,
                [other, after(attn, *behind)],
                place,
            )
            return keep, swap(send, "dp", 1)

        later_keep, later_swap = project_far(FIRST, features - FIRST, own_stay)
        far_keep, far_swap = project_far(0, FIRST, later_keep)
        later_shape = (dest, features - FIRST)
        later_stay, go = call(
            sum_kernel, [shape(later_shape, F32), shape(later_shape, BF16)], [after(later_keep, far_keep), later_swap]
        )
        later_came = to_chip(go, False)
        far_stay, go = call(
            pieces_kernel,
            [shape((2, *first_part), F32), shape((2, *first_part), BF16)],
            [after(far_keep, later_stay), far_swap],
            place,
        )
        far_came = swap(go, "seq", 1)
        last = (half,)
    else:
        attn, carried = call(
            functools.partial(attention_kernel, heads=heads),
            [token_bf16, state_shape],
            [*attend_args, *received],
            place,
        )
        partial = (dot_tn(other, attn) * scale).astype(BF16)
        grad_w = lax.psum_scatter(partial, ("dp", "seq"), scatter_dimension=0, tiled=True).astype(F32)
        last, keep = (), attn

    if paired:
        keep = far_stay
    grad_attn, back = call(
        functools.partial(grad_attn_kernel, heads=heads),
        [token_bf16, state_shape],
        [other, w_out, after(query, keep), column, *last],
        place,
    )

    def pass_back(value, stage):
        return lax.ppermute(value, "seq", [(seq_count - stage, seq_count - 1 - stage)])

    returned = [pass_back(back, 1)] if paired else shift_down(back, seq_count)
    if paired:
        grad_attn = after(grad_attn, back)
    grad_queries, inner_keys, inner_values = call(
        functools.partial(inner_kernel, heads=heads),
        [final((rows, features), BF16), token_f32, token_f32],
        [query, key, value, grad_attn, row, column, weight, carried],
    )
    if paired:
        def chain(stage, *behind):
            (passed,) = call(
                functools.partial(chain_kernel, rows=rows),
                [state_shape],
                [decay, after(back, *behind), returned[-1]],
                place,
            )
            return pass_back(passed, stage)

        returned.append(chain(2, inner_keys))
        later_stay, go = call(
            later_kernel,
            [shape((2, *later_part), F32), shape((2, *later_part), BF16)],
            [own_later, own_later_came, after(later_stay, inner_keys), later_came],
            place,
        )
        later_came = swap(go, "seq", 1)
        far_stay, go = halve(far_stay, far_came, later_stay)
        far_came = swap(go, "seq", 2)
        returned.append(chain(3, far_stay))
        later_stay, go = halve(later_stay, later_came, far_stay)
        later_came = swap(go, "seq", 2)
        first_keep, send = call(
            finish_kernel,
            [shape(first_part, F32), shape(first_part, BF16)],
            [own_stay, own_came, after(far_stay, later_stay), far_came],
            place,
        )
        crossed = swap(send, "dp", 2)
        inner_keys = after(inner_keys, first_keep)
    grad_keys, grad_values = call(
        functools.partial(outer_kernel, heads=heads, chained=paired),
        [final((rows, features), BF16)] * 2,
        [decay, key, value, row, column, inner_keys, inner_values, *returned],
        place,
    )
    if paired:
        (grad_w,) = call(
            result_kernel,
            [final(quarter, F32)],
            [after(first_keep, grad_keys), crossed, later_stay, later_came],
        )
    return grad_queries[None], grad_keys[None], grad_values[None], grad_w


def solution(mesh):
    tokens = P("dp", "seq", "tensor")
    in_specs = (tokens, tokens, tokens, P("dp", "tensor", None), P("tensor", None), tokens)
    out_specs = (tokens, tokens, tokens, P(("dp", "seq"), "tensor"))

    step = jax.shard_map(local, mesh=mesh, in_specs=in_specs, out_specs=out_specs, check_vma=False)
    if not paired_mesh(*(mesh.shape[axis] for axis in ("dp", "seq", "tensor"))):
        return step

    return step
```

```python
import functools
import math

import jax
import jax.numpy as jnp
from jax import lax
from jax.experimental import pallas as pl
from jax.experimental.pallas import tpu as pltpu
from jax.sharding import PartitionSpec as P


F32 = jnp.float32
BF16 = jnp.bfloat16
TILE = 256
FIRST = 256
GRANT = 24 * 1024 * 1024


def dot_nn(a, b):
    return lax.dot_general(a, b, (((1,), (0,)), ((), ())), preferred_element_type=F32)


def dot_nt(a, b):
    return lax.dot_general(a, b, (((1,), (1,)), ((), ())), preferred_element_type=F32)


def dot_tn(a, b):
    return lax.dot_general(a, b, (((0,), (0,)), ((), ())), preferred_element_type=F32)


def call(body, outs, args, scalars=None, scratch=(), near=True):
    count = 0 if scalars is None else 1
    whole = pl.BlockSpec(memory_space=pltpu.VMEM)
    given = whole if near else pl.BlockSpec(memory_space=pltpu.HBM)
    spec = pltpu.PrefetchScalarGridSpec(
        num_scalar_prefetch=count,
        in_specs=[given] * len(args),
        out_specs=[whole] * len(outs),
        scratch_shapes=list(scratch),
    )
    prefix = () if scalars is None else (scalars,)
    args = [pltpu.with_memory_space_constraint(x, pltpu.VMEM if near else pltpu.HBM) for x in args]
    limit = pltpu.CompilerParams(vmem_limit_bytes=GRANT)
    return pl.pallas_call(body, out_shape=list(outs), grid_spec=spec, compiler_params=limit)(*prefix, *args)


def after(value, *others):
    return lax.optimization_barrier((value, *others))[0]


def shape(dims, kind):
    return pltpu.VMEM(dims, kind)


def final(dims, kind):
    return jax.ShapeDtypeStruct(dims, kind)


def running_sum(values):
    length = values.shape[1]
    position = lax.broadcasted_iota(jnp.int32, values.shape, 1)
    step = 1
    while step < length:
        values = values + jnp.where(position >= step, pltpu.roll(values, step, 1), 0.0)
        step *= 2
    return values


def span_decay(decay_ref, start, stop):
    values = decay_ref[...]
    position = lax.broadcasted_iota(jnp.int32, values.shape, 1)
    inside = (position >= start) & (position < stop)
    return jnp.exp(jnp.sum(jnp.where(inside, values, 0.0), axis=1, keepdims=True))


def states_kernel(place, decay_in, query_in, key_in, value_in, *refs, heads):
    *outs, semaphores = refs
    state_ref, row_ref, column_ref, decay_ref, query_ref, key_ref, value_ref = outs
    rows = key_ref.shape[0]
    width = key_ref.shape[1] // heads
    spans = [slice(h * width, (h + 1) * width) for h in range(heads)]
    pairs = ((decay_in, decay_ref), (key_in, key_ref), (value_in, value_ref), (query_in, query_ref))
    copies = [pltpu.make_async_copy(*pair, semaphores.at[n]) for n, pair in enumerate(pairs)]
    for copy in copies:
        copy.start()
    copies[0].wait()
    local = decay_ref[:, pl.ds(pl.multiple_of(place[0] * rows, 128), rows)]
    tall = row_ref.shape[0]
    local = jnp.concatenate([local] * pl.cdiv(tall, heads), axis=0)[:tall]
    cumulative = running_sum(local)
    columns = cumulative.T
    row_ref[...] = cumulative
    column_ref[...] = columns
    copies[1].wait()
    copies[2].wait()
    for h, at in enumerate(spans):
        to_end = jnp.exp(cumulative[h : h + 1, rows - 1 : rows] - columns[:, h : h + 1])
        scaled = (key_ref[:, at].astype(F32) * to_end).astype(BF16)
        state_ref[h] = dot_tn(scaled, value_ref[:, at]).astype(BF16)
    copies[3].wait()


def tiles(rows):
    return [(i, j) for i in range(rows // TILE) for j in range(i + 1)]


def tile_decay(row_ref, column_ref, h, i, j):
    spread = column_ref[i * TILE : (i + 1) * TILE, h : h + 1] - row_ref[h : h + 1, j * TILE : (j + 1) * TILE]
    if i != j:
        return jnp.exp(spread)
    later = lax.broadcasted_iota(jnp.int32, (TILE, TILE), 0)
    earlier = lax.broadcasted_iota(jnp.int32, (TILE, TILE), 1)
    lower = later >= earlier
    return jnp.where(lower, jnp.exp(jnp.where(lower, spread, 0.0)), 0.0)


def weights_kernel(query_ref, key_ref, value_ref, row_ref, column_ref, weight_ref, within_ref, *, heads):
    rows = key_ref.shape[0]
    width = key_ref.shape[1] // heads
    for h in range(heads):
        at = slice(h * width, (h + 1) * width)
        sums = {}
        for n, (i, j) in enumerate(tiles(rows)):
            ti, tj = slice(i * TILE, (i + 1) * TILE), slice(j * TILE, (j + 1) * TILE)
            scores = dot_nt(query_ref[ti, at], key_ref[tj, at])
            weight = (scores * tile_decay(row_ref, column_ref, h, i, j) * (1.0 / width)).astype(BF16)
            weight_ref[h, n] = weight
            term = dot_nn(weight, value_ref[tj, at])
            sums[i] = term if i not in sums else sums[i] + term
        for i, total in sums.items():
            within_ref[i * TILE : (i + 1) * TILE, at] = total


def gather_states(decay_ref, pieces, place, rows, forward):
    factors = []
    for k in range(2, len(pieces) + 1):
        start = (place - k + 1) * rows if forward else (place + 1) * rows
        stop = place * rows if forward else (place + k) * rows
        factors.append(span_decay(decay_ref, start, stop))

    def state(h):
        total = pieces[0][h].astype(F32)
        for factor, piece in zip(factors, pieces[1:], strict=True):
            total = total + factor[h : h + 1] * piece[h].astype(F32)
        return total.astype(BF16)

    return state


def attend(place, decay_ref, query_ref, within_ref, column_ref, pieces, attn_ref, carried_ref, heads):
    rows = query_ref.shape[0]
    width = query_ref.shape[1] // heads
    state = gather_states(decay_ref, pieces, place[0], rows, True)
    for h in range(heads):
        at = slice(h * width, (h + 1) * width)
        carried = state(h)
        carried_ref[h] = carried
        scaled = query_ref[:, at].astype(F32) * (jnp.exp(column_ref[:, h : h + 1]) * (1.0 / width))
        attn_ref[:, at] = (within_ref[:, at] + dot_nn(scaled.astype(BF16), carried)).astype(BF16)


def project(place, grad_ref, attn_ref, send_ref, keep_ref, scale, start=0):
    half, wide = keep_ref.shape
    attn = attn_ref[:, start : start + wide]
    for core, into in ((1 - place[1], send_ref), (place[1], keep_ref)):
        at = pl.ds(pl.multiple_of(core * half, 128), half)
        into[...] = (dot_tn(grad_ref[:, at], attn) * scale).astype(BF16)


def attention_kernel(place, decay_ref, query_ref, within_ref, column_ref, *refs, heads):
    *pieces, attn_ref, carried_ref = refs
    attend(place, decay_ref, query_ref, within_ref, column_ref, pieces, attn_ref, carried_ref, heads)


def attention_project_kernel(place, decay_ref, query_ref, within_ref, column_ref, grad_ref, *refs, heads, scale):
    *pieces, attn_ref, carried_ref, send_ref, keep_ref = refs
    attend(place, decay_ref, query_ref, within_ref, column_ref, pieces, attn_ref, carried_ref, heads)
    project(place, grad_ref, attn_ref, send_ref, keep_ref, scale)


def projection_kernel(place, grad_ref, attn_ref, send_ref, keep_ref, *, scale, start):
    project(place, grad_ref, attn_ref, send_ref, keep_ref, scale, start)


def half_columns(out_ref, index, count):
    return out_ref[:, pl.ds(pl.multiple_of(index * count, 128), count)]


def grad_attn_half_kernel(place, grad_ref, out_ref, total_ref):
    total_ref[...] = dot_nt(grad_ref[...], half_columns(out_ref, place[3], grad_ref.shape[1]))


def grad_attn_kernel(place, grad_ref, out_ref, query_ref, column_ref, *refs, heads):
    *halves, grad_attn_ref, back_ref = refs
    width = query_ref.shape[1] // heads
    if halves:
        total = halves[0][...] + dot_nt(grad_ref[...], half_columns(out_ref, 1 - place[3], grad_ref.shape[1]))
    else:
        total = dot_nt(grad_ref[...], out_ref[...])
    total = total.astype(BF16)
    grad_attn_ref[...] = total
    for h in range(heads):
        at = slice(h * width, (h + 1) * width)
        scaled = query_ref[:, at].astype(F32) * (jnp.exp(column_ref[:, h : h + 1]) * (1.0 / width))
        back_ref[h] = dot_tn(scaled.astype(BF16), total[:, at]).astype(BF16)


def chain_kernel(place, decay_ref, back_ref, came_ref, chain_ref, *, rows):
    factor = span_decay(decay_ref, place[0] * rows, (place[0] + 1) * rows)
    for h in range(back_ref.shape[0]):
        chain_ref[h] = (back_ref[h].astype(F32) + factor[h : h + 1] * came_ref[h].astype(F32)).astype(BF16)


def inner_kernel(
    query_ref, key_ref, value_ref, grad_ref, row_ref, column_ref, weight_ref, carried_ref, dq_ref, dk_ref, dv_ref, *, heads
):
    rows = key_ref.shape[0]
    width = key_ref.shape[1] // heads
    inverse = 1.0 / width
    for h in range(heads):
        at = slice(h * width, (h + 1) * width)
        dq, dk, dv = {}, {}, {}

        def add(store, index, term):
            store[index] = term if index not in store else store[index] + term

        for n, (i, j) in enumerate(tiles(rows)):
            ti, tj = slice(i * TILE, (i + 1) * TILE), slice(j * TILE, (j + 1) * TILE)
            scores = dot_nt(grad_ref[ti, at], value_ref[tj, at])
            weight = (scores * tile_decay(row_ref, column_ref, h, i, j) * inverse).astype(BF16)
            add(dq, i, dot_nn(weight, key_ref[tj, at]))
            add(dk, j, dot_tn(weight, query_ref[ti, at]))
            add(dv, j, dot_tn(weight_ref[h, n], grad_ref[ti, at]))
        for i in range(rows // TILE):
            ti = slice(i * TILE, (i + 1) * TILE)
            scaled = grad_ref[ti, at].astype(F32) * (jnp.exp(column_ref[ti, h : h + 1]) * inverse)
            dq_ref[ti, at] = (dq[i] + dot_nt(scaled.astype(BF16), carried_ref[h])).astype(BF16)
            dk_ref[ti, at] = dk[i]
            dv_ref[ti, at] = dv[i]


def summed_states(pieces):
    def state(h):
        total = pieces[0][h]
        for piece in pieces[1:]:
            total = total + piece[h]
        return total

    return state


def outer_kernel(place, decay_ref, key_ref, value_ref, row_ref, column_ref, inner_k_ref, inner_v_ref, *refs, heads, chained):
    *pieces, dk_ref, dv_ref = refs
    rows = key_ref.shape[0]
    width = key_ref.shape[1] // heads
    state = summed_states(pieces) if chained else gather_states(decay_ref, pieces, place[0], rows, False)
    for h in range(heads):
        at = slice(h * width, (h + 1) * width)
        back = state(h)
        to_end = jnp.exp(row_ref[h : h + 1, rows - 1 : rows] - column_ref[:, h : h + 1])
        values = (value_ref[:, at].astype(F32) * to_end).astype(BF16)
        keys = (key_ref[:, at].astype(F32) * to_end).astype(BF16)
        dk_ref[:, at] = (inner_k_ref[:, at] + dot_nt(values, back)).astype(BF16)
        dv_ref[:, at] = (inner_v_ref[:, at] + dot_nn(keys, back)).astype(BF16)


def owner_turns(bit):
    return (3 - bit, 0, 3, bit)


def sum_kernel(mine_ref, other_ref, keep_ref, send_ref):
    total = mine_ref[...].astype(F32) + other_ref[...].astype(F32)
    keep_ref[...] = total
    send_ref[...] = total.astype(BF16)


def pieces_kernel(place, mine_ref, other_ref, keep_ref, send_ref):
    rows = keep_ref.shape[1]
    for n, turn in enumerate(owner_turns(1)):
        at = pl.ds(pl.multiple_of((place[0] ^ turn) * rows, 16), rows)
        total = mine_ref[at, :].astype(F32) + other_ref[at, :].astype(F32)
        if n < 2:
            keep_ref[n] = total
        else:
            send_ref[n - 2] = total.astype(BF16)


def own_kernel(place, mine_ref, other_ref, keep_ref, send_ref, later_keep_ref, later_send_ref):
    _, rows, wide = keep_ref.shape
    for n, turn in enumerate(owner_turns(1)):
        at = pl.ds(pl.multiple_of((place[0] ^ turn) * rows, 16), rows)
        total = mine_ref[at, :wide].astype(F32) + other_ref[at, :wide].astype(F32)
        if n < 2:
            keep_ref[n] = total
        else:
            send_ref[n - 2] = total.astype(BF16)
    later = mine_ref[:, wide:].astype(F32) + other_ref[:, wide:].astype(F32)
    later_keep_ref[...] = later
    later_send_ref[...] = later.astype(BF16)


def later_kernel(place, own_ref, own_other_ref, far_ref, far_other_ref, keep_ref, send_ref):
    rows = keep_ref.shape[1]
    mine = place[2] == place[3]
    for n, turn in enumerate(owner_turns(1)):
        at = pl.ds(pl.multiple_of((place[0] ^ turn) * rows, 16), rows)
        kept = jnp.where(mine, own_ref[at, :], far_ref[at, :])
        came = jnp.where(mine, own_other_ref[at, :].astype(F32), far_other_ref[at, :].astype(F32))
        if n < 2:
            keep_ref[n] = kept + came
        else:
            send_ref[n - 2] = (kept + came).astype(BF16)


def halve_kernel(mine_ref, other_ref, keep_ref, send_ref):
    send_ref[...] = (mine_ref[0] + other_ref[0].astype(F32)).astype(BF16)
    keep_ref[...] = mine_ref[1] + other_ref[1].astype(F32)


def finish_kernel(place, own_ref, own_other_ref, far_ref, far_other_ref, keep_ref, send_ref):
    own = own_ref[...] + own_other_ref[...].astype(F32)
    far = far_ref[...] + far_other_ref[...].astype(F32)
    mine = place[2] == place[3]
    send_ref[...] = jnp.where(mine, far, own).astype(BF16)
    keep_ref[...] = jnp.where(mine, own, far)


def result_kernel(first_ref, crossed_ref, later_ref, later_other_ref, out_ref):
    wide = first_ref.shape[1]
    out_ref[:, :wide] = first_ref[...] + crossed_ref[...].astype(F32)
    out_ref[:, wide:] = later_ref[...] + later_other_ref[...].astype(F32)


def shift_up(value, count):
    return [lax.ppermute(value, "seq", [(i, i + k) for i in range(count - k)]) for k in range(1, count)]


def shift_down(value, count):
    return [lax.ppermute(value, "seq", [(i, i - k) for i in range(k, count)]) for k in range(1, count)]


def to_chip(value, own):
    tensor_count = lax.axis_size("tensor")
    pairs = []
    for t in range(tensor_count):
        target = t if own else 1 - t
        for core in range(2):
            start = (2 * (1 - target) + core) * tensor_count + t
            pairs.append((start, (2 * target + core) * tensor_count + t))
    return lax.ppermute(value, ("dp", "tensor"), pairs)


def swap(value, axis, bit):
    return lax.ppermute(value, axis, [(i, i ^ bit) for i in range(lax.axis_size(axis))])


def paired_mesh(dp_count, seq_count, tensor_count):
    return tensor_count == 2 and dp_count == 2 * tensor_count and seq_count == 4


def local(queries, key_vectors, value_vectors, log_decay, w_out, grad_out):
    micro, rows, features = queries.shape
    heads = log_decay.shape[1]
    width = features // heads
    dp_count, seq_count, tensor_count = (lax.axis_size(n) for n in ("dp", "seq", "tensor"))
    seq_index, dp_index, tensor_index = (lax.axis_index(n) for n in ("seq", "dp", "tensor"))
    scale = 1.0 / math.sqrt(micro * dp_count * rows * seq_count)
    query, key, value = queries[0], key_vectors[0], value_vectors[0]
    decay, grad = log_decay[0], grad_out[0]
    columns = grad.shape[1]
    paired = paired_mesh(dp_count, seq_count, tensor_count)
    place = jnp.stack([seq_index, dp_index % 2, dp_index // 2, tensor_index]).astype(jnp.int32)
    tall = -(-heads // 8) * 8
    state_shape = shape((heads, width, width), BF16)
    token_f32, token_bf16 = shape((rows, features), F32), shape((rows, features), BF16)

    if paired:
        other = swap(grad, "tensor", 1)
    else:
        other = lax.all_gather(grad, "tensor", axis=1, tiled=True)

    state, row, column, decay, query, key, value = call(
        functools.partial(states_kernel, heads=heads),
        [state_shape, shape((tall, rows), F32), shape((rows, tall), F32), shape(decay.shape, F32)] + [token_bf16] * 3,
        [decay, query, key, value],
        place,
        [pltpu.SemaphoreType.DMA((4,))],
        near=False,
    )
    received = shift_up(state, seq_count)
    weight, within = call(
        functools.partial(weights_kernel, heads=heads),
        [shape((heads, len(tiles(rows)), TILE, TILE), BF16), token_f32],
        [query, key, value, row, column],
    )
    attend_args = [decay, query, within, column]

    if paired:
        dest = columns // 2
        piece = dest // seq_count
        parts = [shape((dest, features), BF16)] * 2

        quarter = (piece, features)

        first_part, later_part = (piece, FIRST), (piece, features - FIRST)

        def halve(stay, came, *behind):
            dims = stay.shape[1:]
            return call(halve_kernel, [shape(dims, F32), shape(dims, BF16)], [after(stay, *behind), came])

        attn, carried, send, keep = call(
            functools.partial(attention_project_kernel, heads=heads, scale=scale),
            [token_bf16, state_shape, *parts],
            [*attend_args, grad, *received],
            place,
        )
        own_swap = swap(send, "dp", 1)
        own_stay, go, own_later, later_go = call(
            own_kernel,
            [
                shape((2, *first_part), F32),
                shape((2, *first_part), BF16),
                shape((dest, features - FIRST), F32),
                shape((dest, features - FIRST), BF16),
            ],
            [keep, own_swap],
            place,
        )
        own_came = swap(go, "seq", 1)
        own_later_came = to_chip(later_go, True)
        (half,) = call(grad_attn_half_kernel, [token_f32], [grad, after(w_out, own_stay)], place)

        own_stay, go = halve(own_stay, own_came, half)
        own_came = swap(go, "seq", 2)

        def project_far(start, width, *behind):
            send, keep = call(
                functools.partial(projection_kernel, scale=scale, start=start),
                [shape((dest, width), BF16)] * 2,
                [other, after(attn, *behind)],
                place,
            )
            return keep, swap(send, "dp", 1)

        later_keep, later_swap = project_far(FIRST, features - FIRST, own_stay)
        far_keep, far_swap = project_far(0, FIRST, later_keep)
        later_shape = (dest, features - FIRST)
        later_stay, go = call(
            sum_kernel, [shape(later_shape, F32), shape(later_shape, BF16)], [after(later_keep, far_keep), later_swap]
        )
        later_came = to_chip(go, False)
        far_stay, go = call(
            pieces_kernel,
            [shape((2, *first_part), F32), shape((2, *first_part), BF16)],
            [after(far_keep, later_stay), far_swap],
            place,
        )
        far_came = swap(go, "seq", 1)
        last = (half,)
    else:
        attn, carried = call(
            functools.partial(attention_kernel, heads=heads),
            [token_bf16, state_shape],
            [*attend_args, *received],
            place,
        )
        partial = (dot_tn(other, attn) * scale).astype(BF16)
        grad_w = lax.psum_scatter(partial, ("dp", "seq"), scatter_dimension=0, tiled=True).astype(F32)
        last, keep = (), attn

    if paired:
        keep = far_stay
    grad_attn, back = call(
        functools.partial(grad_attn_kernel, heads=heads),
        [token_bf16, state_shape],
        [other, w_out, after(query, keep), column, *last],
        place,
    )

    def pass_back(value, stage):
        return lax.ppermute(value, "seq", [(seq_count - stage, seq_count - 1 - stage)])

    returned = [pass_back(back, 1)] if paired else shift_down(back, seq_count)
    if paired:
        def chain(stage, *behind):
            (passed,) = call(
                functools.partial(chain_kernel, rows=rows),
                [state_shape],
                [decay, after(back, *behind), returned[-1]],
                place,
            )
            return pass_back(passed, stage)

        far_stay, go = halve(far_stay, far_came, back)
        far_came = swap(go, "seq", 2)
        later_stay, go = call(
            later_kernel,
            [shape((2, *later_part), F32), shape((2, *later_part), BF16)],
            [own_later, own_later_came, after(later_stay, far_stay), later_came],
            place,
        )
        later_came = swap(go, "seq", 1)
        returned.append(chain(2, later_stay))
        grad_attn = after(grad_attn, later_stay)
    grad_queries, inner_keys, inner_values = call(
        functools.partial(inner_kernel, heads=heads),
        [final((rows, features), BF16), token_f32, token_f32],
        [query, key, value, grad_attn, row, column, weight, carried],
    )
    if paired:
        returned.append(chain(3, inner_keys))
        later_stay, go = halve(later_stay, later_came, inner_keys)
        later_came = swap(go, "seq", 2)
        first_keep, send = call(
            finish_kernel,
            [shape(first_part, F32), shape(first_part, BF16)],
            [own_stay, own_came, after(far_stay, later_stay), far_came],
            place,
        )
        crossed = swap(send, "dp", 2)
        inner_keys = after(inner_keys, first_keep)
    grad_keys, grad_values = call(
        functools.partial(outer_kernel, heads=heads, chained=paired),
        [final((rows, features), BF16)] * 2,
        [decay, key, value, row, column, inner_keys, inner_values, *returned],
        place,
    )
    if paired:
        (grad_w,) = call(
            result_kernel,
            [final(quarter, F32)],
            [after(first_keep, grad_keys), crossed, later_stay, later_came],
        )
    return grad_queries[None], grad_keys[None], grad_values[None], grad_w


def solution(mesh):
    tokens = P("dp", "seq", "tensor")
    in_specs = (tokens, tokens, tokens, P("dp", "tensor", None), P("tensor", None), tokens)
    out_specs = (tokens, tokens, tokens, P(("dp", "seq"), "tensor"))

    step = jax.shard_map(local, mesh=mesh, in_specs=in_specs, out_specs=out_specs, check_vma=False)
    if not paired_mesh(*(mesh.shape[axis] for axis in ("dp", "seq", "tensor"))):
        return step

    return step
```
